32 devices in a mesh: groups: 2 (over y), blk: 4 (over x, core), narrow: 4 (over z).
Axes of the slice: x: 2, y: 2, z: 4, core: 2. Of those that a mesh axis runs over, the one named last changes fastest.
Arguments:
- tokens: bfloat16 [8192, 1024], P(('groups', 'blk', 'narrow')), parts along dimension 0, may hold values from -64 to 64
- latents: bfloat16 [2048, 1024], P('blk'), may hold values from -48 to 48
- cotangent: bfloat16 [4096, 1024], P(('groups', 'blk')), parts along dimension 0, may hold values from -6 to 6
- query_weight: bfloat16 [1024, 1024], replicated, may hold values from -0.1875 to 0.1875
- keyvalue_weight: bfloat16 [1024, 2048], replicated, may hold values from -0.1875 to 0.1875
- counts: int32 [8, 4], P(('groups', 'blk')), parts along dimension 0, may hold values from 1 to 256, 614 in all within a row
Outputs:
- latent_out: bfloat16 [4096, 1024], P(('groups', 'blk')), parts along dimension 0
- grad_latents: bfloat16 [4096, 1024], P(('groups', 'blk')), parts along dimension 0
- grad_query_weight: bfloat16 [2048, 1024], P('groups', 'narrow'), parts along dimension 0
- grad_tokens: bfloat16 [8192, 1024], P(('groups', 'blk', 'narrow')), parts along dimension 0
The draws below stay inside these ranges and needn't reach their ends.
There are 2 independent parts, one for each index of `groups`. The reference program is written for one: setup_inputs(seed, part) draws one part's arguments, and reference() takes and returns one part's arrays. A program takes and returns all parts, laid end to end along the dimension named above; an argument that names none is the same for every part. Nothing has to cross between parts.
Inputs may be any that keep to these rules, and one draw needn't show every extreme that they name: Each row of counts sums to 614 and has an entry equal to 256.
All inputs are finite; a program needn't handle non-finite values.
Results may differ from the reference program's by a relative error of at most 0.0102.
The reference program's roundings to bfloat16 on the way (of `queries`, `pairs`, `weights`, `dscore`, `query_low` and `pair_grad`) count: a program that leaves them out, or rounds other values in their place, can miss the bound.
Values may be sent and summed in bfloat16 or wider, within the bound.
No kernel may reach another device: no remote copies, remote signals or barrier semaphores. Data moves between devices by JAX's collectives and lax.ppermute only.
A program may use at most 128 MiB of HBM per device.

```python
import math
import jax
import jax.numpy as jnp
import numpy as np
from jax import lax

D = 1024
HEADS = 16
NL = 2048
TOK_DEV = 256
HEAD = 64
TOKENS = 4096
VALID = 614
N_BLK = 4
N_NARROW = 4


def scaled_rows(key, row_count, col_count, strength, rarity):
    key_one = jax.random.fold_in(key, 0)
    key_three = jax.random.fold_in(key, 2)
    key_four = jax.random.fold_in(key, 3)
    drawn = jnp.clip(jax.random.normal(key_one, (row_count, col_count), jnp.float32), -6.0, 6.0)
    row_place = jnp.arange(row_count)[:, None]
    strong_rows = (jax.random.randint(key_three, (row_count, 1), 0, rarity) == 0) | (row_place == 0)
    levels = (2 + jax.random.randint(key_four, (row_count, 1), 0, 3)).astype(jnp.float32) * 0.25
    drawn = drawn * jnp.where(strong_rows, strength * levels, 1.0)
    return drawn.astype(jnp.bfloat16)


def draw_tokens(key, part):
    return scaled_rows(jax.random.fold_in(key, 11), TOKENS, D, 6.0, 128)


def draw_latents(key, part):
    return scaled_rows(jax.random.fold_in(key, 23), NL, D, 5.0, 32)


def shard_levels(stream_key, extent, pieces, low, largest):
    factor_of, own = 1.0, jax.random.fold_in(stream_key, 6)
    for axis_at, parts in pieces:
        steps = jnp.exp(jax.random.uniform(jax.random.fold_in(own, axis_at), (parts,), jnp.float32, low / len(pieces), largest / len(pieces)))
        factor_of = factor_of * jnp.repeat(steps, extent[axis_at] // parts).reshape([-1 if axis == axis_at else 1 for axis in range(len(extent))])
    return factor_of


def profile(amount, total, limit, lean):
    weights = [(1 << 20) // math.isqrt(grade ** lean) + 1 for grade in range(2, amount + 1)]
    spare, given = total - limit - (amount - 1), [1] * (amount - 1)
    while spare > 0:
        free = [i for i in range(amount - 1) if given[i] < limit]
        mass, remaining = sum([weights[i] for i in free]), spare
        for i in free:
            extra = min(limit - given[i], max(1, remaining * weights[i] // mass), spare)
            given[i] = given[i] + extra
            spare = spare - extra
    return np.array([limit] + given)


def ragged_sizes(own_key, count, total, limit, skew):
    if count == 2:
        one = jax.random.randint(own_key, (), max(1, total - limit), min(limit, total - 1) + 1)
        return jnp.stack([one, total - one])
    sizes = jnp.asarray(profile(count, total, limit, skew), jnp.int32)
    twos = (count - 1) // 2
    source_of, sink = sizes[1:1 + 2 * twos:2], sizes[2:2 + 2 * twos:2]
    slack = jnp.minimum(source_of - 1, limit - sink)
    moved = jax.random.randint(jax.random.fold_in(own_key, 1), (twos,), 0, 1 << 20) % (slack + 1)
    sizes = sizes.at[1:1 + 2 * twos:2].set(source_of - moved).at[2:2 + 2 * twos:2].set(sink + moved)
    return sizes[jax.random.permutation(jax.random.fold_in(own_key, 2), count)]


def normal_values(key, dims, spread, most, shards=(), kind=jnp.bfloat16):
    values = jax.random.normal(key, dims, jnp.float32) * spread
    if len(shards) > 0:
        values = shard_levels(key, dims, shards, -0.22, 0.18) * values
    return jnp.clip(values, min=-most, max=most).astype(kind)


def setup_inputs(seed: int = 0, part: int = 0) -> dict:
    key_of = jax.random.split(jax.random.key(seed), 7)
    part_splits = jax.random.split(jax.random.fold_in(key_of[6], part), 7)
    tokens = draw_tokens(jax.random.fold_in(jax.random.fold_in(key_of[6], part), 71), part)
    latents = draw_latents(jax.random.fold_in(key_of[6], 71), part)
    cotangent = normal_values(part_splits[2], (NL, D), 1.0, 6.0, ((0, 4),))
    query_weight = normal_values(key_of[3], (D, D), D ** -0.5, 0.1875)
    keyvalue_weight = normal_values(key_of[4], (D, 2 * D), D ** -0.5, 0.1875)
    counts = jax.vmap(lambda own: ragged_sizes(own, N_NARROW, VALID, TOK_DEV, 2))(jax.random.split(part_splits[5], N_BLK)).reshape((N_BLK, N_NARROW)).astype(jnp.int32)
    return dict(tokens=tokens, latents=latents, cotangent=cotangent, query_weight=query_weight, keyvalue_weight=keyvalue_weight, counts=counts)


NEG = -1e30


def by_heads(matrix):
    return matrix.reshape(matrix.shape[0], HEADS, HEAD).transpose(1, 0, 2)


def join_heads(stacked):
    return stacked.transpose(1, 0, 2).reshape(stacked.shape[1], HEADS * HEAD)


def reference(tokens, latents, cotangent, query_weight, keyvalue_weight, counts):
    valid_mask = (jnp.arange(TOK_DEV, dtype=jnp.int32)[None, :] < counts.reshape(-1)[:, None].astype(jnp.int32)).reshape(-1)
    queries = jnp.dot(latents, query_weight, preferred_element_type=jnp.float32).astype(jnp.bfloat16)
    pairs = jnp.dot(tokens, keyvalue_weight, preferred_element_type=jnp.float32).astype(jnp.bfloat16)
    factor = HEAD ** -0.5

    def one_head(group):
        query_h, key_h, value_h, grad_h = group
        scores = jnp.dot(query_h, key_h.T, preferred_element_type=jnp.float32) * factor
        scores = jnp.where(valid_mask[None, :], scores, NEG)
        row_max = jnp.max(scores, axis=1)
        powers = jnp.exp(scores - row_max[:, None])
        row_sum = jnp.sum(powers, axis=1)
        attended = jnp.dot(powers.astype(jnp.bfloat16), value_h, preferred_element_type=jnp.float32) / row_sum[:, None]
        log_total = row_max + jnp.log(row_sum)
        probs = jnp.exp(scores - log_total[:, None])
        delta = jnp.sum(grad_h.astype(jnp.float32) * attended, axis=1)
        dprob = jnp.dot(grad_h, value_h.T, preferred_element_type=jnp.float32)
        dscore = (probs * (dprob - delta[:, None]) * factor).astype(jnp.bfloat16)
        query_grad = jnp.dot(dscore, key_h, preferred_element_type=jnp.float32)
        key_grad = jnp.dot(dscore.T, query_h, preferred_element_type=jnp.float32)
        value_grad = jnp.dot(probs.astype(jnp.bfloat16).T, grad_h, preferred_element_type=jnp.float32)
        return attended, query_grad, key_grad, value_grad

    attended, query_grad, key_grad, value_grad = lax.map(
        one_head, (by_heads(queries), by_heads(pairs[:, :D]), by_heads(pairs[:, D:]), by_heads(cotangent)))
    latent_out = join_heads(attended).astype(jnp.bfloat16)
    query_low = join_heads(query_grad).astype(jnp.bfloat16)
    pair_grad = jnp.concatenate([join_heads(key_grad), join_heads(value_grad)], axis=1).astype(jnp.bfloat16)
    grad_tokens = jnp.dot(pair_grad, keyvalue_weight.T, preferred_element_type=jnp.float32).astype(jnp.bfloat16)
    grad_latents = jnp.dot(query_low, query_weight.T, preferred_element_type=jnp.float32).astype(jnp.bfloat16)
    grad_query_weight = jnp.dot(latents.T, query_low, preferred_element_type=jnp.float32).astype(jnp.bfloat16)
    return latent_out, grad_latents, grad_query_weight, grad_tokens
```

```python
import functools

import jax
import jax.numpy as jnp
from jax import lax
from jax.experimental import pallas as pl
from jax.experimental.pallas import tpu as pltpu
from jax.sharding import PartitionSpec as P

HEADS = 16
HEAD = 64


NEG = -1e30


def shifted(shard, axis, by):
    length = lax.axis_size(axis)
    return lax.ppermute(shard, axis, [(i, (i + by) % length) for i in range(length)])


def merged_2(shard, axis, combine):
    everything = jax.tree.map(lambda part: lax.all_gather(part, axis), shard)
    initial = jax.tree.map(lambda part: part[0], everything)

    def turn(k, so_far):
        return combine(so_far, jax.tree.map(lambda part: part[k], everything))

    return lax.fori_loop(1, lax.axis_size(axis), turn, initial)


def attend_forward(queries, row_max, row_sum, weighted, key_heads, value_heads, valid_mask):
    latent_rows, col_count = queries.shape
    heads_here = key_heads.shape[1]
    head_size = key_heads.shape[2]
    query_heads = queries.reshape(latent_rows, heads_here, head_size)
    scores = jnp.einsum(
        "qhd,khd->hqk", query_heads, key_heads, preferred_element_type=jnp.float32
    ) * head_size ** (-0.5)
    scores = jnp.where(valid_mask[None, None, :], scores, NEG)
    new_max = jnp.maximum(row_max, jnp.max(scores, axis=2))
    powers = jnp.exp(scores - new_max[:, :, None])
    rescale = jnp.exp(row_max - new_max)
    row_sum = row_sum * rescale + jnp.sum(powers, axis=2)
    update = jnp.einsum(
        "hqk,khd->qhd", powers.astype(jnp.bfloat16), value_heads, preferred_element_type=jnp.float32
    )
    weighted = weighted.reshape(latent_rows, heads_here, head_size) * rescale.T[:, :, None] + update
    return (new_max, row_sum, weighted.reshape(latent_rows, col_count))


def join_partials(earlier, latter):
    max_one, sum_one, acc_one = earlier
    max_two, sum_two, acc_two = latter
    new_max = jnp.maximum(max_one, max_two)
    scale_one = jnp.exp(max_one - new_max)
    scale_two = jnp.exp(max_two - new_max)
    latent_rows = acc_one.shape[0]
    heads_here = max_one.shape[0]
    merged = (
        acc_one.reshape(latent_rows, heads_here, -1) * scale_one.T[:, :, None]
        + acc_two.reshape(latent_rows, heads_here, -1) * scale_two.T[:, :, None]
    )
    return (new_max, sum_one * scale_one + sum_two * scale_two, merged.reshape(latent_rows, -1))


def attend_backward(queries, grads, log_total, delta, key_heads, value_heads, valid_mask):
    latent_rows, col_count = queries.shape
    heads_here = key_heads.shape[1]
    head_size = key_heads.shape[2]
    factor = head_size ** (-0.5)
    query_heads = queries.reshape(latent_rows, heads_here, head_size)
    grad_heads = grads.reshape(latent_rows, heads_here, head_size)
    scores = (
        jnp.einsum("qhd,khd->hqk", query_heads, key_heads, preferred_element_type=jnp.float32)
        * factor
    )
    scores = jnp.where(valid_mask[None, None, :], scores, NEG)
    probs = jnp.exp(scores - log_total[:, :, None])
    dprob = jnp.einsum("qhd,khd->hqk", grad_heads, value_heads, preferred_element_type=jnp.float32)
    dscore = (probs * (dprob - delta[:, :, None]) * factor).astype(jnp.bfloat16)
    query_term = jnp.einsum("hqk,khd->qhd", dscore, key_heads, preferred_element_type=jnp.float32)
    key_term = jnp.einsum("hqk,qhd->khd", dscore, query_heads, preferred_element_type=jnp.float32)
    value_term = jnp.einsum(
        "hqk,qhd->khd", probs.astype(jnp.bfloat16), grad_heads, preferred_element_type=jnp.float32
    )
    return (
        query_term.reshape(latent_rows, col_count),
        key_term.reshape(-1, col_count),
        value_term.reshape(-1, col_count),
    )


def forward_cycle(queries, key_heads, value_heads, valid_mask):
    latent_rows, col_count = queries.shape
    heads_here = key_heads.shape[1]
    initial = (
        queries,
        jnp.full((heads_here, latent_rows), NEG, jnp.float32),
        jnp.zeros((heads_here, latent_rows), jnp.float32),
        jnp.zeros((latent_rows, col_count), jnp.float32),
    )

    def forward_cycle_step(carried, unused):
        current, row_max, row_sum, weighted = carried
        row_max, row_sum, weighted = attend_forward(
            current, row_max, row_sum, weighted, key_heads, value_heads, valid_mask
        )
        moved = shifted(current, "blk", 1)
        row_max, row_sum, weighted = shifted((row_max, row_sum, weighted), "blk", 1)
        return ((moved, row_max, row_sum, weighted), current)

    final, visited = lax.scan(forward_cycle_step, initial, None, length=lax.axis_size("blk"))
    return (final[1], final[2], final[3], visited)


def backward_cycle(visited, grad_share, log_total, delta, key_heads, value_heads, valid_mask):
    latent_rows, col_count = grad_share.shape
    token_count = key_heads.shape[0]
    initial = (
        grad_share,
        log_total,
        delta,
        jnp.zeros((latent_rows, col_count), jnp.float32),
        jnp.zeros((token_count, col_count), jnp.float32),
        jnp.zeros((token_count, col_count), jnp.float32),
    )

    def backward_cycle_step(carried, queries):
        grads, log_here, delta_here, query_grad, key_grad, value_grad = carried
        query_term, key_term, value_term = attend_backward(
            queries, grads, log_here, delta_here, key_heads, value_heads, valid_mask
        )
        moved = shifted(grads, "blk", 1)
        log_here, delta_here, query_grad = shifted(
            (log_here, delta_here, query_grad + query_term), "blk", 1
        )
        return (
            (moved, log_here, delta_here, query_grad, key_grad + key_term, value_grad + value_term),
            None,
        )

    final, unused = lax.scan(backward_cycle_step, initial, visited)
    return (final[3], final[4], final[5])


NT = (((1,), (1,)), ((), ()))
NN = (((1,), (0,)), ((), ()))
LOG2E = 1.4426950408889634


def mm(one, two, dims=NN):
    return lax.dot_general(one, two, dims, preferred_element_type=jnp.float32)


def whole(shape):
    return pl.BlockSpec(shape, lambda *unused: (0,) * len(shape))


def pairs_kernel(tok_ref, key_w_ref, value_w_ref, out_ref, *, heads):
    tok = tok_ref[...]
    keys = mm(tok, key_w_ref[...]).astype(jnp.bfloat16)
    values = mm(tok, value_w_ref[...]).astype(jnp.bfloat16)
    for h in range(heads):
        cols = slice(h * HEAD, (h + 1) * HEAD)
        out_ref[h, 0] = jnp.concatenate([keys[:, cols], values[:, cols]], axis=1)


def project_pairs(tokens, weight, groups):
    rows, width = tokens.shape
    cols = width // groups
    heads = cols // HEAD
    return pl.pallas_call(
        functools.partial(pairs_kernel, heads=heads),
        grid=(groups,),
        in_specs=[
            whole((rows, width)),
            pl.BlockSpec((width, cols), lambda n: (0, n)),
            pl.BlockSpec((width, cols), lambda n: (0, n + groups)),
        ],
        out_specs=pl.BlockSpec((heads, 1, rows, 2 * HEAD), lambda n: (0, n, 0, 0)),
        out_shape=jax.ShapeDtypeStruct((heads, groups, rows, 2 * HEAD), jnp.bfloat16),
        name="project_pairs",
    )(tokens, weight, weight)


def queries_kernel(index_ref, lat_ref, w_ref, grad_ref, out_ref, *, heads):
    queries = mm(lat_ref[...], w_ref[...]).astype(jnp.bfloat16)
    grads = grad_ref[...]
    for h in range(heads):
        cols = slice(h * HEAD, (h + 1) * HEAD)
        out_ref[h] = jnp.concatenate([queries[:, cols], grads[:, cols]], axis=1)


def project_queries(latents, weight, cotangent, index, groups):
    rows, width = latents.shape
    cols = width // groups
    heads = cols // HEAD
    return pl.pallas_call(
        functools.partial(queries_kernel, heads=heads),
        grid_spec=pltpu.PrefetchScalarGridSpec(
            num_scalar_prefetch=1,
            grid=(1,),
            in_specs=[
                pl.BlockSpec((rows, width), lambda i, at: (0, 0)),
                pl.BlockSpec((width, cols), lambda i, at: (0, at[0])),
                pl.BlockSpec((rows, cols), lambda i, at: (0, at[0])),
            ],
            out_specs=pl.BlockSpec((heads, rows, 2 * HEAD), lambda i, at: (0, 0, 0)),
        ),
        out_shape=jax.ShapeDtypeStruct((heads, rows, 2 * HEAD), jnp.bfloat16),
        name="project_queries",
    )(index, latents, weight, cotangent)


def attention_kernel(
    counts_ref, kv_ref, qg_ref, og_ref, dkv_ref, wide, kv, kvt, scores, acc, *, valid, tile
):
    step = pl.program_id(0)
    sources, slot, width = kv_ref.shape
    block = qg_ref.shape[0]
    padded = kv.shape[0]
    factor = HEAD ** (-0.5)
    row8 = lax.broadcasted_iota(jnp.int32, (8, width), 0)

    @pl.when(step == 0)
    def _():
        at = jnp.int32(0)
        for s in range(sources):
            offset = at % 8
            base = pl.multiple_of(at - offset, 8)
            rows = kv_ref[s].astype(jnp.float32)
            rows = jnp.concatenate([rows, jnp.zeros((8, width), jnp.float32)], axis=0)
            rows = pltpu.roll(rows, offset, 0)
            earlier = wide[pl.ds(base, 8), :]
            wide[pl.ds(base, 8), :] = jnp.where(row8 < offset, earlier, rows[:8])
            wide[pl.ds(base + 8, slot), :] = rows[8:]
            at = at + counts_ref[s]
        for t in range(0, padded, tile):
            size = min(tile, padded - t)
            part = wide[t:t + size, :]
            if t + size > valid:
                part = jnp.where(
                    lax.broadcasted_iota(jnp.int32, (size, width), 0) < valid - t, part, 0.0
                )
            kv[t:t + size, :] = part.astype(jnp.bfloat16)
            kvt[:, t:t + size] = part.T.astype(jnp.bfloat16)
        acc[...] = jnp.zeros(acc.shape, jnp.float32)

    qg = qg_ref[...]
    lane = lax.broadcasted_iota(jnp.int32, (block, width), 1)
    zero = jnp.zeros_like(qg)
    query = jnp.where(lane < HEAD, qg, zero)
    grad = jnp.where(lane < HEAD, zero, qg)
    grad_t = qg.astype(jnp.float32).T[HEAD:, :]
    tiles = [(t, min(tile, padded - t)) for t in range(0, padded, tile)]
    highest = jnp.full((8, block), NEG, jnp.float32)
    for t, size in tiles:
        part = mm(kv[t:t + size, :], query, NT)
        if t + size > valid:
            part = jnp.where(
                lax.broadcasted_iota(jnp.int32, (size, block), 0) < valid - t, part, NEG
            )
        scores[t:t + size, :] = part
        highest = jnp.maximum(highest, jnp.max(part.reshape(size // 8, 8, block), axis=0))
    top = jnp.max(highest, axis=0, keepdims=True)
    total = jnp.zeros((8, block), jnp.float32)
    out_t = jnp.zeros((HEAD, block), jnp.float32)
    for t, size in tiles:
        power = jnp.exp2((scores[t:t + size, :] - top) * (factor * LOG2E))
        scores[t:t + size, :] = power
        total = total + jnp.sum(power.reshape(size // 8, 8, block), axis=0)
        out_t = out_t + mm(kvt[HEAD:, t:t + size], power.astype(jnp.bfloat16))
    inverse = 1.0 / jnp.sum(total, axis=0, keepdims=True)
    out_t = out_t * inverse
    delta = jnp.sum(grad_t * out_t, axis=0, keepdims=True)
    query_t = jnp.zeros((HEAD, block), jnp.float32)
    for t, size in tiles:
        dprob = mm(kv[t:t + size, :], grad, NT)
        prob = scores[t:t + size, :] * inverse
        dscore = (prob * (dprob - delta)).astype(jnp.bfloat16)
        acc[t:t + size, :] += mm(dscore, query) + mm(prob.astype(jnp.bfloat16), grad)
        query_t = query_t + mm(kvt[:HEAD, t:t + size], dscore)
    both = jnp.concatenate([out_t, query_t * factor], axis=0)
    og_ref[...] = both.T.astype(jnp.bfloat16)

    @pl.when(step == pl.num_programs(0) - 1)
    def _():
        scale = jnp.where(
            lax.broadcasted_iota(jnp.int32, (slot, width), 1) < HEAD, factor, 1.0
        )
        row = lax.broadcasted_iota(jnp.int32, (slot, width), 0)
        at = jnp.int32(0)
        for s in range(sources):
            count = counts_ref[s]
            offset = at % 8
            base = pl.multiple_of(at - offset, 8)
            rows = pltpu.roll(acc[pl.ds(base, slot + 8), :], (slot + 8 - offset) % (slot + 8), 0)
            dkv_ref[s] = jnp.where(row < count, rows[:slot] * scale, 0.0).astype(jnp.bfloat16)
            at = at + count


def attention(counts, kv, qg, valid, block=256, tile=256):
    sources, slot, width = kv.shape
    latent_rows = qg.shape[0]
    padded = -(-valid // 128) * 128
    room = padded + slot + 16
    return pl.pallas_call(
        functools.partial(attention_kernel, valid=valid, tile=tile),
        grid_spec=pltpu.PrefetchScalarGridSpec(
            num_scalar_prefetch=1,
            grid=(latent_rows // block,),
            in_specs=[
                pl.BlockSpec((sources, slot, width), lambda i, c: (0, 0, 0)),
                pl.BlockSpec((block, width), lambda i, c: (i, 0)),
            ],
            out_specs=[
                pl.BlockSpec((block, width), lambda i, c: (i, 0)),
                pl.BlockSpec((sources, slot, width), lambda i, c: (0, 0, 0)),
            ],
            scratch_shapes=[
                pltpu.VMEM((room, width), jnp.float32),
                pltpu.VMEM((padded, width), jnp.bfloat16),
                pltpu.VMEM((width, padded), jnp.bfloat16),
                pltpu.VMEM((padded, block), jnp.float32),
                pltpu.VMEM((room, width), jnp.float32),
            ],
        ),
        out_shape=[
            jax.ShapeDtypeStruct((latent_rows, width), jnp.bfloat16),
            jax.ShapeDtypeStruct((sources, slot, width), jnp.bfloat16),
        ],
        name="attention",
    )(counts, kv, qg)


def side_by_side(ref_part, heads, first):
    lanes = slice(0, HEAD) if first else slice(HEAD, 2 * HEAD)
    return jnp.concatenate([ref_part[h][:, lanes] for h in range(heads)], axis=1)


def token_grad_kernel(dkv_ref, key_w_ref, value_w_ref, out_ref, acc, *, heads):
    step = pl.program_id(0)

    @pl.when(step == 0)
    def _():
        acc[...] = jnp.zeros(acc.shape, jnp.float32)

    part = dkv_ref[0]
    keys = side_by_side(part, heads, True)
    values = side_by_side(part, heads, False)
    acc[...] += mm(keys, key_w_ref[...], NT) + mm(values, value_w_ref[...], NT)

    @pl.when(step == pl.num_programs(0) - 1)
    def _():
        out_ref[...] = acc[...].astype(jnp.bfloat16)


def token_grad(dkv, weight):
    groups, heads, rows, pair = dkv.shape
    width = weight.shape[0]
    cols = heads * HEAD
    return pl.pallas_call(
        functools.partial(token_grad_kernel, heads=heads),
        grid=(groups,),
        in_specs=[
            pl.BlockSpec((1, heads, rows, pair), lambda n: (n, 0, 0, 0)),
            pl.BlockSpec((width, cols), lambda n: (0, n)),
            pl.BlockSpec((width, cols), lambda n: (0, n + groups)),
        ],
        out_specs=whole((rows, width)),
        out_shape=jax.ShapeDtypeStruct((rows, width), jnp.bfloat16),
        scratch_shapes=[pltpu.VMEM((rows, width), jnp.float32)],
        name="token_grad",
    )(dkv, weight, weight)


def latent_grad_kernel(og_ref, w_ref, out_ref, grad_ref, acc, *, heads):
    step = pl.program_id(0)

    @pl.when(step == 0)
    def _():
        acc[...] = jnp.zeros(acc.shape, jnp.float32)

    part = og_ref[0]
    out_ref[...] = side_by_side(part, heads, True)
    acc[...] += mm(side_by_side(part, heads, False), w_ref[...], NT)

    @pl.when(step == pl.num_programs(0) - 1)
    def _():
        grad_ref[...] = acc[...].astype(jnp.bfloat16)


def latent_grad(og, weight):
    groups, heads, rows, pair = og.shape
    width = weight.shape[0]
    cols = heads * HEAD
    return pl.pallas_call(
        functools.partial(latent_grad_kernel, heads=heads),
        grid=(groups,),
        in_specs=[
            pl.BlockSpec((1, heads, rows, pair), lambda n: (n, 0, 0, 0)),
            pl.BlockSpec((width, cols), lambda n: (0, n)),
        ],
        out_specs=[pl.BlockSpec((rows, cols), lambda n: (0, n)), whole((rows, width))],
        out_shape=[
            jax.ShapeDtypeStruct((rows, width), jnp.bfloat16),
            jax.ShapeDtypeStruct((rows, width), jnp.bfloat16),
        ],
        scratch_shapes=[pltpu.VMEM((rows, width), jnp.float32)],
        name="latent_grad",
    )(og, weight)


def weight_grad_kernel(lat_ref, og_ref, out_ref, *, heads):
    low = side_by_side(og_ref[...], heads, False)
    out_ref[...] = lax.dot_general(
        lat_ref[...], low, (((0,), (0,)), ((), ())), preferred_element_type=jnp.float32
    )


def weight_grad(latents, og):
    rows, width = latents.shape
    heads, _, pair = og.shape
    cols = heads * HEAD
    return pl.pallas_call(
        functools.partial(weight_grad_kernel, heads=heads),
        out_shape=jax.ShapeDtypeStruct((width, cols), jnp.float32),
        name="weight_grad",
    )(latents, og)


def by_head(tokens, latents, cotangent, query_weight, keyvalue_weight, counts):
    blocks = lax.axis_size("blk")
    groups = lax.axis_size("narrow")
    everyone = ("blk", "narrow")
    tok_rows, width = tokens.shape
    latent_rows = latents.shape[0]
    valid = tok_rows * groups * 614 // 1024 * blocks
    index = lax.axis_index("narrow").astype(jnp.int32).reshape(1)
    all_counts = lax.all_to_all(
        jnp.broadcast_to(counts, (blocks, groups)), "blk", 0, 0, tiled=True
    ).reshape(blocks * groups)
    pairs = project_pairs(tokens, keyvalue_weight, groups)
    pairs = pairs.reshape(blocks * groups, tok_rows, 2 * HEAD)
    pairs = lax.all_to_all(pairs, everyone, 0, 0, tiled=True)
    qg = project_queries(latents, query_weight, cotangent, index, groups)
    qg = lax.all_to_all(qg, "blk", 0, 0, tiled=True)
    og, dkv = attention(all_counts, pairs, qg.reshape(blocks * latent_rows, 2 * HEAD), valid)
    dkv = lax.all_to_all(dkv, everyone, 0, 0, tiled=True)
    dkv = dkv.reshape(blocks, groups, tok_rows, 2 * HEAD).transpose(1, 0, 2, 3)
    grad_tokens = token_grad(dkv, keyvalue_weight)
    og = lax.all_to_all(og.reshape(blocks, latent_rows, 2 * HEAD), "blk", 0, 0, tiled=True)
    weight_part = weight_grad(latents, og)
    weight_part = lax.all_to_all(weight_part.reshape(blocks, width // blocks, -1), "blk", 0, 0)
    weight_part = jnp.sum(weight_part, axis=0).astype(jnp.bfloat16)
    grad_query_weight = lax.all_to_all(
        jnp.broadcast_to(weight_part, (blocks,) + weight_part.shape), "blk", 0, 0
    ).reshape(width, -1)
    every_og = lax.all_to_all(
        jnp.broadcast_to(og, (groups,) + og.shape), "narrow", 0, 0, tiled=False
    )
    latent_out, grad_latents = latent_grad(every_og, query_weight)
    return (latent_out, grad_latents, grad_query_weight, grad_tokens)


def on_device(tokens, latents, cotangent, query_weight, keyvalue_weight, counts):
    narrow_size = lax.axis_size("narrow")
    narrow_index = lax.axis_index("narrow")
    tok_rows = tokens.shape[0]
    model_width = tokens.shape[1]
    share = model_width // narrow_size
    queries = jnp.dot(latents, query_weight, preferred_element_type=jnp.float32).astype(
        jnp.bfloat16
    )
    pairs = jnp.dot(tokens, keyvalue_weight, preferred_element_type=jnp.float32).astype(
        jnp.bfloat16
    )
    key_heads = pairs[:, :model_width].reshape(tok_rows, HEADS, HEAD)
    value_heads = pairs[:, model_width:].reshape(tok_rows, HEADS, HEAD)
    valid_mask = jnp.arange(tok_rows) < counts[0, narrow_index]
    row_max, row_sum, weighted, visited = forward_cycle(queries, key_heads, value_heads, valid_mask)
    row_max, row_sum, weighted = merged_2((row_max, row_sum, weighted), "narrow", join_partials)
    heads_here = row_max.shape[0]
    latent_rows = weighted.shape[0]
    attended = weighted.reshape(latent_rows, heads_here, HEAD) / row_sum.T[:, :, None]
    attended_low = attended.reshape(latent_rows, -1).astype(jnp.bfloat16)
    delta = jnp.sum(
        cotangent.astype(jnp.float32).reshape(latent_rows, heads_here, HEAD) * attended, axis=2
    ).T
    log_total = row_max + jnp.log(row_sum)
    query_grad, key_grad, value_grad = backward_cycle(
        visited, cotangent, log_total, delta, key_heads, value_heads, valid_mask
    )
    pair_grad = jnp.concatenate([key_grad, value_grad], axis=1).astype(jnp.bfloat16)
    query_part = lax.psum_scatter(query_grad, "narrow", scatter_dimension=1, tiled=True)
    query_low = query_part.astype(jnp.bfloat16)
    weight_cols = lax.dynamic_slice_in_dim(query_weight, narrow_index * share, share, 1)
    weight_term = lax.dot_general(
        latents, query_low, (((0,), (0,)), ((), ())), preferred_element_type=jnp.float32
    )
    grad_query_weight = lax.psum(weight_term, "blk").astype(jnp.bfloat16)
    latent_term = lax.dot_general(
        query_low, weight_cols, (((1,), (1,)), ((), ())), preferred_element_type=jnp.float32
    )
    grad_latents = lax.psum(latent_term, "narrow").astype(jnp.bfloat16)
    grad_tokens = lax.dot_general(
        pair_grad, keyvalue_weight, (((1,), (1,)), ((), ())), preferred_element_type=jnp.float32
    ).astype(jnp.bfloat16)
    return (attended_low, grad_latents, grad_query_weight, grad_tokens)


def solution(mesh):
    placed = (
        P(("groups", "blk", "narrow"), None),
        P("blk", None),
        P(("groups", "blk"), None),
        P(),
        P(),
        P(("groups", "blk"), None),
    )
    one_head_each = mesh.shape["blk"] * mesh.shape["narrow"] == HEADS
    return jax.shard_map(
        by_head if one_head_each else on_device,
        mesh=mesh,
        in_specs=placed,
        out_specs=(
            P(("groups", "blk"), None),
            P(("groups", "blk"), None),
            P("groups", "narrow"),
            P(("groups", "blk", "narrow"), None),
        ),
        check_vma=False,
    )
```

```python
import functools

import jax
import jax.numpy as jnp
from jax import lax
from jax.experimental import pallas as pl
from jax.experimental.pallas import tpu as pltpu
from jax.sharding import PartitionSpec as P

HEADS = 16
HEAD = 64


NEG = -1e30


def shifted(shard, axis, by):
    length = lax.axis_size(axis)
    return lax.ppermute(shard, axis, [(i, (i + by) % length) for i in range(length)])


def merged_2(shard, axis, combine):
    everything = jax.tree.map(lambda part: lax.all_gather(part, axis), shard)
    initial = jax.tree.map(lambda part: part[0], everything)

    def turn(k, so_far):
        return combine(so_far, jax.tree.map(lambda part: part[k], everything))

    return lax.fori_loop(1, lax.axis_size(axis), turn, initial)


def attend_forward(queries, row_max, row_sum, weighted, key_heads, value_heads, valid_mask):
    latent_rows, col_count = queries.shape
    heads_here = key_heads.shape[1]
    head_size = key_heads.shape[2]
    query_heads = queries.reshape(latent_rows, heads_here, head_size)
    scores = jnp.einsum(
        "qhd,khd->hqk", query_heads, key_heads, preferred_element_type=jnp.float32
    ) * head_size ** (-0.5)
    scores = jnp.where(valid_mask[None, None, :], scores, NEG)
    new_max = jnp.maximum(row_max, jnp.max(scores, axis=2))
    powers = jnp.exp(scores - new_max[:, :, None])
    rescale = jnp.exp(row_max - new_max)
    row_sum = row_sum * rescale + jnp.sum(powers, axis=2)
    update = jnp.einsum(
        "hqk,khd->qhd", powers.astype(jnp.bfloat16), value_heads, preferred_element_type=jnp.float32
    )
    weighted = weighted.reshape(latent_rows, heads_here, head_size) * rescale.T[:, :, None] + update
    return (new_max, row_sum, weighted.reshape(latent_rows, col_count))


def join_partials(earlier, latter):
    max_one, sum_one, acc_one = earlier
    max_two, sum_two, acc_two = latter
    new_max = jnp.maximum(max_one, max_two)
    scale_one = jnp.exp(max_one - new_max)
    scale_two = jnp.exp(max_two - new_max)
    latent_rows = acc_one.shape[0]
    heads_here = max_one.shape[0]
    merged = (
        acc_one.reshape(latent_rows, heads_here, -1) * scale_one.T[:, :, None]
        + acc_two.reshape(latent_rows, heads_here, -1) * scale_two.T[:, :, None]
    )
    return (new_max, sum_one * scale_one + sum_two * scale_two, merged.reshape(latent_rows, -1))


def attend_backward(queries, grads, log_total, delta, key_heads, value_heads, valid_mask):
    latent_rows, col_count = queries.shape
    heads_here = key_heads.shape[1]
    head_size = key_heads.shape[2]
    factor = head_size ** (-0.5)
    query_heads = queries.reshape(latent_rows, heads_here, head_size)
    grad_heads = grads.reshape(latent_rows, heads_here, head_size)
    scores = (
        jnp.einsum("qhd,khd->hqk", query_heads, key_heads, preferred_element_type=jnp.float32)
        * factor
    )
    scores = jnp.where(valid_mask[None, None, :], scores, NEG)
    probs = jnp.exp(scores - log_total[:, :, None])
    dprob = jnp.einsum("qhd,khd->hqk", grad_heads, value_heads, preferred_element_type=jnp.float32)
    dscore = (probs * (dprob - delta[:, :, None]) * factor).astype(jnp.bfloat16)
    query_term = jnp.einsum("hqk,khd->qhd", dscore, key_heads, preferred_element_type=jnp.float32)
    key_term = jnp.einsum("hqk,qhd->khd", dscore, query_heads, preferred_element_type=jnp.float32)
    value_term = jnp.einsum(
        "hqk,qhd->khd", probs.astype(jnp.bfloat16), grad_heads, preferred_element_type=jnp.float32
    )
    return (
        query_term.reshape(latent_rows, col_count),
        key_term.reshape(-1, col_count),
        value_term.reshape(-1, col_count),
    )


def forward_cycle(queries, key_heads, value_heads, valid_mask):
    latent_rows, col_count = queries.shape
    heads_here = key_heads.shape[1]
    initial = (
        queries,
        jnp.full((heads_here, latent_rows), NEG, jnp.float32),
        jnp.zeros((heads_here, latent_rows), jnp.float32),
        jnp.zeros((latent_rows, col_count), jnp.float32),
    )

    def forward_cycle_step(carried, unused):
        current, row_max, row_sum, weighted = carried
        row_max, row_sum, weighted = attend_forward(
            current, row_max, row_sum, weighted, key_heads, value_heads, valid_mask
        )
        moved = shifted(current, "blk", 1)
        row_max, row_sum, weighted = shifted((row_max, row_sum, weighted), "blk", 1)
        return ((moved, row_max, row_sum, weighted), current)

    final, visited = lax.scan(forward_cycle_step, initial, None, length=lax.axis_size("blk"))
    return (final[1], final[2], final[3], visited)


def backward_cycle(visited, grad_share, log_total, delta, key_heads, value_heads, valid_mask):
    latent_rows, col_count = grad_share.shape
    token_count = key_heads.shape[0]
    initial = (
        grad_share,
        log_total,
        delta,
        jnp.zeros((latent_rows, col_count), jnp.float32),
        jnp.zeros((token_count, col_count), jnp.float32),
        jnp.zeros((token_count, col_count), jnp.float32),
    )

    def backward_cycle_step(carried, queries):
        grads, log_here, delta_here, query_grad, key_grad, value_grad = carried
        query_term, key_term, value_term = attend_backward(
            queries, grads, log_here, delta_here, key_heads, value_heads, valid_mask
        )
        moved = shifted(grads, "blk", 1)
        log_here, delta_here, query_grad = shifted(
            (log_here, delta_here, query_grad + query_term), "blk", 1
        )
        return (
            (moved, log_here, delta_here, query_grad, key_grad + key_term, value_grad + value_term),
            None,
        )

    final, unused = lax.scan(backward_cycle_step, initial, visited)
    return (final[3], final[4], final[5])


NT = (((1,), (1,)), ((), ()))
NN = (((1,), (0,)), ((), ()))
LOG2E = 1.4426950408889634


def mm(one, two, dims=NN):
    return lax.dot_general(one, two, dims, preferred_element_type=jnp.float32)


def whole(shape):
    return pl.BlockSpec(shape, lambda *unused: (0,) * len(shape))


def pairs_kernel(tok_ref, key_w_ref, value_w_ref, out_ref, *, heads):
    tok = tok_ref[...]
    keys = mm(tok, key_w_ref[...]).astype(jnp.bfloat16)
    values = mm(tok, value_w_ref[...]).astype(jnp.bfloat16)
    for h in range(heads):
        cols = slice(h * HEAD, (h + 1) * HEAD)
        out_ref[h, 0] = jnp.concatenate([keys[:, cols], values[:, cols]], axis=1)


def project_pairs(tokens, weight, groups):
    rows, width = tokens.shape
    cols = width // groups
    heads = cols // HEAD
    return pl.pallas_call(
        functools.partial(pairs_kernel, heads=heads),
        grid=(groups,),
        in_specs=[
            whole((rows, width)),
            pl.BlockSpec((width, cols), lambda n: (0, n)),
            pl.BlockSpec((width, cols), lambda n: (0, n + groups)),
        ],
        out_specs=pl.BlockSpec((heads, 1, rows, 2 * HEAD), lambda n: (0, n, 0, 0)),
        out_shape=jax.ShapeDtypeStruct((heads, groups, rows, 2 * HEAD), jnp.bfloat16),
        name="project_pairs",
    )(tokens, weight, weight)


def queries_kernel(
    index_ref, counts_ref, lat_ref, w_ref, grad_ref, out_ref, queries, *, heads, extra
):
    step = pl.program_id(0)
    rows = grad_ref.shape[0]

    @pl.when(step == 0)
    def _():
        queries[...] = mm(lat_ref[...], w_ref[...]).astype(jnp.bfloat16)

    lane = lax.broadcasted_iota(jnp.int32, (extra, 2 * HEAD), 1)
    counts = jnp.zeros((extra, 2 * HEAD), jnp.float32)
    for n in range(counts_ref.shape[0]):
        counts = jnp.where(lane == n, counts_ref[n].astype(jnp.float32), counts)
    out_ref[0, rows:, :] = counts.astype(jnp.bfloat16)
    for h in range(heads):
        cols = slice(h * HEAD, (h + 1) * HEAD)

        @pl.when(step == h)
        def _(cols=cols):
            out_ref[0, :rows, :] = jnp.concatenate([queries[:, cols], grad_ref[:, cols]], axis=1)


def project_queries(latents, weight, cotangent, index, counts, groups, extra=16):
    rows, width = latents.shape
    cols = width // groups
    heads = cols // HEAD
    return pl.pallas_call(
        functools.partial(queries_kernel, heads=heads, extra=extra),
        grid_spec=pltpu.PrefetchScalarGridSpec(
            num_scalar_prefetch=2,
            grid=(heads,),
            in_specs=[
                pl.BlockSpec((rows, width), lambda i, at, c: (0, 0)),
                pl.BlockSpec((width, cols), lambda i, at, c: (0, at[0])),
                pl.BlockSpec((rows, cols), lambda i, at, c: (0, at[0])),
            ],
            out_specs=pl.BlockSpec(
                (1, rows + extra, 2 * HEAD), lambda i, at, c: (i ^ at[1], 0, 0)
            ),
            scratch_shapes=[pltpu.VMEM((rows, cols), jnp.bfloat16)],
        ),
        out_shape=jax.ShapeDtypeStruct((heads, rows + extra, 2 * HEAD), jnp.bfloat16),
        name="project_queries",
    )(index, counts, latents, weight, cotangent)


def count_of(counts_ref, index_ref, source):
    return counts_ref[source // 4 ^ index_ref[1], source % 4]


def pack_tokens(counts_ref, index_ref, kv_ref, wide, kv, kvt, valid, tile):
    sources, slot, width = kv_ref.shape
    padded = kv.shape[0]
    row8 = lax.broadcasted_iota(jnp.int32, (8, width), 0)
    at = jnp.int32(0)
    for s in range(sources):
        offset = at % 8
        base = pl.multiple_of(at - offset, 8)
        rows = kv_ref[s].astype(jnp.float32)
        rows = jnp.concatenate([rows, jnp.zeros((8, width), jnp.float32)], axis=0)
        rows = pltpu.roll(rows, offset, 0)
        earlier = wide[pl.ds(base, 8), :]
        wide[pl.ds(base, 8), :] = jnp.where(row8 < offset, earlier, rows[:8])
        wide[pl.ds(base + 8, slot), :] = rows[8:]
        at = at + count_of(counts_ref, index_ref, s)
    for t in range(0, padded, tile):
        size = min(tile, padded - t)
        part = wide[t:t + size, :]
        if t + size > valid:
            part = jnp.where(
                lax.broadcasted_iota(jnp.int32, (size, width), 0) < valid - t, part, 0.0
            )
        kv[t:t + size, :] = part.astype(jnp.bfloat16)
        kvt[:, t:t + size] = part.T.astype(jnp.bfloat16)


def unpack_tokens(counts_ref, index_ref, acc, dkv_ref):
    sources, slot, width = dkv_ref.shape
    scale = jnp.where(
        lax.broadcasted_iota(jnp.int32, (slot, width), 1) < HEAD, HEAD ** (-0.5), 1.0
    )
    row = lax.broadcasted_iota(jnp.int32, (slot, width), 0)
    at = jnp.int32(0)
    for s in range(sources):
        count = count_of(counts_ref, index_ref, s)
        offset = at % 8
        base = pl.multiple_of(at - offset, 8)
        rows = pltpu.roll(acc[pl.ds(base, slot + 8), :], (slot + 8 - offset) % (slot + 8), 0)
        dkv_ref[s] = jnp.where(row < count, rows[:slot] * scale, 0.0).astype(jnp.bfloat16)
        at = at + count


def attend_block(qg, kv, kvt, scores, acc, valid, tile):
    block, width = qg.shape
    padded = kv.shape[0]
    factor = HEAD ** (-0.5)
    lane = lax.broadcasted_iota(jnp.int32, (block, width), 1)
    zero = jnp.zeros_like(qg)
    query = jnp.where(lane < HEAD, qg, zero)
    grad = jnp.where(lane < HEAD, zero, qg)
    grad_t = qg.astype(jnp.float32).T[HEAD:, :]
    tiles = [(t, min(tile, padded - t)) for t in range(0, padded, tile)]
    highest = jnp.full((8, block), NEG, jnp.float32)
    for t, size in tiles:
        part = mm(kv[t:t + size, :], query, NT)
        if t + size > valid:
            part = jnp.where(
                lax.broadcasted_iota(jnp.int32, (size, block), 0) < valid - t, part, NEG
            )
        scores[t:t + size, :] = part
        highest = jnp.maximum(highest, jnp.max(part.reshape(size // 8, 8, block), axis=0))
    top = jnp.max(highest, axis=0, keepdims=True)
    total = jnp.zeros((8, block), jnp.float32)
    out_t = jnp.zeros((HEAD, block), jnp.float32)
    for t, size in tiles:
        power = jnp.exp2((scores[t:t + size, :] - top) * (factor * LOG2E))
        scores[t:t + size, :] = power
        total = total + jnp.sum(power.reshape(size // 8, 8, block), axis=0)
        out_t = out_t + mm(kvt[HEAD:, t:t + size], power.astype(jnp.bfloat16))
    inverse = 1.0 / jnp.sum(total, axis=0, keepdims=True)
    out_t = out_t * inverse
    delta = jnp.sum(grad_t * out_t, axis=0, keepdims=True)
    query_t = jnp.zeros((HEAD, block), jnp.float32)
    for t, size in tiles:
        dprob = mm(kv[t:t + size, :], grad, NT)
        prob = scores[t:t + size, :] * inverse
        dscore = (prob * (dprob - delta)).astype(jnp.bfloat16)
        acc[t:t + size, :] += mm(dscore, query) + mm(prob.astype(jnp.bfloat16), grad)
        query_t = query_t + mm(kvt[:HEAD, t:t + size], dscore)
    both = jnp.concatenate([out_t, query_t * factor], axis=0)
    return both.T.astype(jnp.bfloat16)


def first_kernel(
    counts_ref, index_ref, kv_ref, qg_ref, og_ref, kv, kvt, acc, wide, scores, *, valid, tile
):
    @pl.when(pl.program_id(0) == 0)
    def _():
        pack_tokens(counts_ref, index_ref, kv_ref, wide, kv, kvt, valid, tile)
        acc[...] = jnp.zeros(acc.shape, jnp.float32)

    og_ref[0] = attend_block(qg_ref[0], kv, kvt, scores, acc, valid, tile)


def later_kernel(
    counts_ref,
    index_ref,
    kv,
    kvt,
    acc_ref,
    qg_ref,
    og_ref,
    out_ref,
    acc,
    scores,
    *,
    valid,
    tile,
    last,
):
    @pl.when(pl.program_id(0) == 0)
    def _():
        acc[...] = acc_ref[...]

    og_ref[0] = attend_block(qg_ref[0], kv, kvt, scores, acc, valid, tile)

    @pl.when(pl.program_id(0) == pl.num_programs(0) - 1)
    def _():
        if last:
            unpack_tokens(counts_ref, index_ref, acc, out_ref)
        else:
            out_ref[...] = acc[...]


def attention(counts, index, kv, qg, valid, latent_rows, chunks, tile=256):
    sources, slot, width = kv.shape
    blocks = qg.shape[0]
    block = latent_rows // chunks
    padded = -(-valid // 128) * 128
    room = padded + slot + 16
    packed = [
        jax.ShapeDtypeStruct((padded, width), jnp.bfloat16),
        jax.ShapeDtypeStruct((width, padded), jnp.bfloat16),
    ]
    acc_shape = jax.ShapeDtypeStruct((room, width), jnp.float32)
    og_shape = jax.ShapeDtypeStruct((blocks, block, width), jnp.bfloat16)
    wide = pltpu.VMEM((room, width), jnp.float32)
    scores = pltpu.VMEM((padded, block), jnp.float32)
    og_spec = pl.BlockSpec((1, block, width), lambda i, c, at: (i, 0, 0))
    cost = pl.CostEstimate(
        flops=24 * blocks * block * padded * 256,
        transcendentals=blocks * block * padded,
        bytes_accessed=4 * room * width * 3,
    )
    outs = []
    for j in range(chunks):
        last = j == chunks - 1
        qg_spec = pl.BlockSpec((1, block, width), lambda i, c, at, j=j: (i, j, 0))
        if j == 0:
            og, key_value, key_value_t, acc = pl.pallas_call(
                functools.partial(first_kernel, valid=valid, tile=tile),
                grid_spec=pltpu.PrefetchScalarGridSpec(
                    num_scalar_prefetch=2,
                    grid=(blocks,),
                    in_specs=[whole(kv.shape), qg_spec],
                    out_specs=[og_spec] + [whole(s.shape) for s in packed + [acc_shape]],
                    scratch_shapes=[wide, scores],
                ),
                out_shape=[og_shape] + packed + [acc_shape],
                cost_estimate=cost,
                name="attention_first",
            )(counts, index, kv, qg)
        else:
            out_shape = jax.ShapeDtypeStruct(kv.shape, jnp.bfloat16) if last else acc_shape
            og, acc = pl.pallas_call(
                functools.partial(later_kernel, valid=valid, tile=tile, last=last),
                grid_spec=pltpu.PrefetchScalarGridSpec(
                    num_scalar_prefetch=2,
                    grid=(blocks,),
                    in_specs=[whole(s.shape) for s in packed + [acc_shape]] + [qg_spec],
                    out_specs=[og_spec, whole(out_shape.shape)],
                    scratch_shapes=[wide, scores],
                ),
                out_shape=[og_shape, out_shape],
                cost_estimate=cost,
                name="attention_later",
            )(counts, index, key_value, key_value_t, acc, qg)
        outs.append(og)
    return outs, acc


def side_by_side(part, heads, first, flip=0):
    lanes = slice(0, HEAD) if first else slice(HEAD, 2 * HEAD)
    return jnp.concatenate([part[h ^ flip][:, lanes] for h in range(heads)], axis=1)


def token_grad_kernel(dkv_ref, key_w_ref, value_w_ref, out_ref, acc, *, heads):
    step = pl.program_id(0)

    @pl.when(step == 0)
    def _():
        acc[...] = jnp.zeros(acc.shape, jnp.float32)

    part = [dkv_ref[h, 0] for h in range(heads)]
    keys = side_by_side(part, heads, True)
    values = side_by_side(part, heads, False)
    acc[...] += mm(keys, key_w_ref[...], NT) + mm(values, value_w_ref[...], NT)

    @pl.when(step == pl.num_programs(0) - 1)
    def _():
        out_ref[...] = acc[...].astype(jnp.bfloat16)


def token_grad(dkv, weight):
    heads, groups, rows, pair = dkv.shape
    width = weight.shape[0]
    cols = heads * HEAD
    return pl.pallas_call(
        functools.partial(token_grad_kernel, heads=heads),
        grid=(groups,),
        in_specs=[
            pl.BlockSpec((heads, 1, rows, pair), lambda n: (0, n, 0, 0)),
            pl.BlockSpec((width, cols), lambda n: (0, n)),
            pl.BlockSpec((width, cols), lambda n: (0, n + groups)),
        ],
        out_specs=whole((rows, width)),
        out_shape=jax.ShapeDtypeStruct((rows, width), jnp.bfloat16),
        scratch_shapes=[pltpu.VMEM((rows, width), jnp.float32)],
        name="token_grad",
    )(dkv, weight, weight)


def latent_grad_kernel(index_ref, *refs, heads, groups):
    w_ref = refs[groups]
    out_ref, grad_ref = refs[-2:]
    cols = heads * HEAD
    total = None
    for k in range(groups):
        part = refs[k]
        at = pl.multiple_of((index_ref[0] ^ k) * cols, cols)
        out_ref[:, pl.ds(at, cols)] = side_by_side(part, heads, True, index_ref[1])
        term = mm(side_by_side(part, heads, False, index_ref[1]), w_ref[:, pl.ds(at, cols)], NT)
        total = term if total is None else total + term
    grad_ref[...] = total.astype(jnp.bfloat16)


def latent_grad(index, parts, weight, chunk, chunks, earlier):
    heads, rows, pair = parts[0].shape
    groups = len(parts)
    width = weight.shape[0]
    shape = jax.ShapeDtypeStruct((rows * chunks, width), jnp.bfloat16)
    part_spec = pl.BlockSpec((heads, rows, pair), lambda i, at: (0, 0, 0))
    out_spec = pl.BlockSpec((rows, width), lambda i, at: (chunk, 0))
    return pl.pallas_call(
        functools.partial(latent_grad_kernel, heads=heads, groups=groups),
        grid_spec=pltpu.PrefetchScalarGridSpec(
            num_scalar_prefetch=1,
            grid=(1,),
            in_specs=[part_spec] * groups
            + [pl.BlockSpec(weight.shape, lambda i, at: (0, 0))]
            + [pl.BlockSpec(memory_space=pl.ANY)] * len(earlier),
            out_specs=[out_spec, out_spec],
        ),
        out_shape=[shape, shape],
        input_output_aliases={2 + groups + k: k for k in range(len(earlier))},
        name="latent_grad",
    )(index, *parts, weight, *earlier)


def weight_grad_kernel(*refs, slots):
    out_ref = refs[-1]
    total = None
    for k in range(slots):
        at = 0
        for og_ref in refs[slots:-1]:
            rows = og_ref.shape[1]
            low = og_ref[k].astype(jnp.float32).T[HEAD:, :].astype(jnp.bfloat16)
            term = mm(low, refs[k][at:at + rows, :])
            total = term if total is None else total + term
            at = at + rows
    out_ref[...] = total.astype(jnp.bfloat16)


def weight_grad(latents, outs):
    width = latents[0].shape[1]
    return pl.pallas_call(
        functools.partial(weight_grad_kernel, slots=len(latents)),
        out_shape=jax.ShapeDtypeStruct((HEAD, width), jnp.bfloat16),
        name="weight_grad",
    )(*latents, *outs)


def turn_kernel(index_ref, *refs):
    out_ref, scratch = refs[-2:]
    for k, ref in enumerate(refs[:-2]):
        at = pl.multiple_of((index_ref[1] ^ k) * HEAD, HEAD)
        scratch[pl.ds(at, HEAD), :] = ref[...].astype(jnp.float32)
    out_ref[...] = scratch[...].T.astype(jnp.bfloat16)


def turn(index, parts):
    width = parts[0].shape[1]
    cols = HEAD * len(parts)
    spec = pl.BlockSpec((HEAD, width), lambda i, at: (0, 0))
    return pl.pallas_call(
        turn_kernel,
        grid_spec=pltpu.PrefetchScalarGridSpec(
            num_scalar_prefetch=1,
            grid=(1,),
            in_specs=[spec] * len(parts),
            out_specs=pl.BlockSpec((width, cols), lambda i, at: (0, 0)),
            scratch_shapes=[pltpu.VMEM((cols, width), jnp.float32)],
        ),
        out_shape=jax.ShapeDtypeStruct((width, cols), jnp.bfloat16),
        name="turn",
    )(index, *parts)


def swapped(shard, axis, bit):
    return lax.ppermute(shard, axis, [(i, i ^ bit) for i in range(lax.axis_size(axis))])


def exchanged(slots, axis):
    others = [swapped(slots[k], axis, k) for k in range(1, slots.shape[0])]
    return jnp.stack([slots[0]] + others)


def gathered(shard, axis):
    near = swapped(shard, axis, 1)
    far = swapped(shard, axis, 2)
    return [shard, near, far, swapped(far, axis, 1)]


def by_head(tokens, latents, cotangent, query_weight, keyvalue_weight, counts):
    blocks = lax.axis_size("blk")
    groups = lax.axis_size("narrow")
    everyone = ("blk", "narrow")
    tok_rows, width = tokens.shape
    latent_rows = latents.shape[0]
    chunks = 2
    valid = tok_rows * groups * 614 // 1024 * blocks
    index = jnp.stack([lax.axis_index("narrow"), lax.axis_index("blk")]).astype(jnp.int32)
    pairs = project_pairs(tokens, keyvalue_weight, groups)
    pairs = pairs.reshape(blocks * groups, tok_rows, 2 * HEAD)
    held, pairs = lax.optimization_barrier((latents, pairs))
    pairs = lax.all_to_all(pairs, everyone, 0, 0, tiled=True)
    qg = project_queries(held, query_weight, cotangent, index, counts.reshape(groups), groups)
    qg = exchanged(qg, "blk")
    all_counts = qg[:, latent_rows, :groups].astype(jnp.int32)
    held, qg = lax.optimization_barrier((latents, qg))
    every = gathered(held, "blk")
    outs, dkv = attention(all_counts, index, pairs, qg, valid, latent_rows, chunks)
    parts = [gathered(exchanged(og, "blk"), "narrow") for og in outs]
    dkv = lax.all_to_all(dkv, everyone, 0, 0, tiled=True)
    grad_tokens = token_grad(
        dkv.reshape(blocks, groups, tok_rows, 2 * HEAD), keyvalue_weight
    )
    grad_query_weight = turn(index, gathered(weight_grad(every, outs), "blk"))
    done = ()
    for j in range(chunks):
        done = latent_grad(index, parts[j], query_weight, j, chunks, done)
    latent_out, grad_latents = done
    return (latent_out, grad_latents, grad_query_weight, grad_tokens)


def on_device(tokens, latents, cotangent, query_weight, keyvalue_weight, counts):
    narrow_size = lax.axis_size("narrow")
    narrow_index = lax.axis_index("narrow")
    tok_rows = tokens.shape[0]
    model_width = tokens.shape[1]
    share = model_width // narrow_size
    queries = jnp.dot(latents, query_weight, preferred_element_type=jnp.float32).astype(
        jnp.bfloat16
    )
    pairs = jnp.dot(tokens, keyvalue_weight, preferred_element_type=jnp.float32).astype(
        jnp.bfloat16
    )
    key_heads = pairs[:, :model_width].reshape(tok_rows, HEADS, HEAD)
    value_heads = pairs[:, model_width:].reshape(tok_rows, HEADS, HEAD)
    valid_mask = jnp.arange(tok_rows) < counts[0, narrow_index]
    row_max, row_sum, weighted, visited = forward_cycle(queries, key_heads, value_heads, valid_mask)
    row_max, row_sum, weighted = merged_2((row_max, row_sum, weighted), "narrow", join_partials)
    heads_here = row_max.shape[0]
    latent_rows = weighted.shape[0]
    attended = weighted.reshape(latent_rows, heads_here, HEAD) / row_sum.T[:, :, None]
    attended_low = attended.reshape(latent_rows, -1).astype(jnp.bfloat16)
    delta = jnp.sum(
        cotangent.astype(jnp.float32).reshape(latent_rows, heads_here, HEAD) * attended, axis=2
    ).T
    log_total = row_max + jnp.log(row_sum)
    query_grad, key_grad, value_grad = backward_cycle(
        visited, cotangent, log_total, delta, key_heads, value_heads, valid_mask
    )
    pair_grad = jnp.concatenate([key_grad, value_grad], axis=1).astype(jnp.bfloat16)
    query_part = lax.psum_scatter(query_grad, "narrow", scatter_dimension=1, tiled=True)
    query_low = query_part.astype(jnp.bfloat16)
    weight_cols = lax.dynamic_slice_in_dim(query_weight, narrow_index * share, share, 1)
    weight_term = lax.dot_general(
        latents, query_low, (((0,), (0,)), ((), ())), preferred_element_type=jnp.float32
    )
    grad_query_weight = lax.psum(weight_term, "blk").astype(jnp.bfloat16)
    latent_term = lax.dot_general(
        query_low, weight_cols, (((1,), (1,)), ((), ())), preferred_element_type=jnp.float32
    )
    grad_latents = lax.psum(latent_term, "narrow").astype(jnp.bfloat16)
    grad_tokens = lax.dot_general(
        pair_grad, keyvalue_weight, (((1,), (1,)), ((), ())), preferred_element_type=jnp.float32
    ).astype(jnp.bfloat16)
    return (attended_low, grad_latents, grad_query_weight, grad_tokens)


def solution(mesh):
    placed = (
        P(("groups", "blk", "narrow"), None),
        P("blk", None),
        P(("groups", "blk"), None),
        P(),
        P(),
        P(("groups", "blk"), None),
    )
    one_head_each = mesh.shape["blk"] == 4 and mesh.shape["narrow"] == 4
    return jax.shard_map(
        by_head if one_head_each else on_device,
        mesh=mesh,
        in_specs=placed,
        out_specs=(
            P(("groups", "blk"), None),
            P(("groups", "blk"), None),
            P("groups", "narrow"),
            P(("groups", "blk", "narrow"), None),
        ),
        check_vma=False,
    )
```

```python
import functools

import jax
import jax.numpy as jnp
from jax import lax
from jax.experimental import pallas as pl
from jax.experimental.pallas import tpu as pltpu
from jax.sharding import PartitionSpec as P

HEADS = 16
HEAD = 64


NEG = -1e30


def shifted(shard, axis, by):
    length = lax.axis_size(axis)
    return lax.ppermute(shard, axis, [(i, (i + by) % length) for i in range(length)])


def merged_2(shard, axis, combine):
    everything = jax.tree.map(lambda part: lax.all_gather(part, axis), shard)
    initial = jax.tree.map(lambda part: part[0], everything)

    def turn(k, so_far):
        return combine(so_far, jax.tree.map(lambda part: part[k], everything))

    return lax.fori_loop(1, lax.axis_size(axis), turn, initial)


def attend_forward(queries, row_max, row_sum, weighted, key_heads, value_heads, valid_mask):
    latent_rows, col_count = queries.shape
    heads_here = key_heads.shape[1]
    head_size = key_heads.shape[2]
    query_heads = queries.reshape(latent_rows, heads_here, head_size)
    scores = jnp.einsum(
        "qhd,khd->hqk", query_heads, key_heads, preferred_element_type=jnp.float32
    ) * head_size ** (-0.5)
    scores = jnp.where(valid_mask[None, None, :], scores, NEG)
    new_max = jnp.maximum(row_max, jnp.max(scores, axis=2))
    powers = jnp.exp(scores - new_max[:, :, None])
    rescale = jnp.exp(row_max - new_max)
    row_sum = row_sum * rescale + jnp.sum(powers, axis=2)
    update = jnp.einsum(
        "hqk,khd->qhd", powers.astype(jnp.bfloat16), value_heads, preferred_element_type=jnp.float32
    )
    weighted = weighted.reshape(latent_rows, heads_here, head_size) * rescale.T[:, :, None] + update
    return (new_max, row_sum, weighted.reshape(latent_rows, col_count))


def join_partials(earlier, latter):
    max_one, sum_one, acc_one = earlier
    max_two, sum_two, acc_two = latter
    new_max = jnp.maximum(max_one, max_two)
    scale_one = jnp.exp(max_one - new_max)
    scale_two = jnp.exp(max_two - new_max)
    latent_rows = acc_one.shape[0]
    heads_here = max_one.shape[0]
    merged = (
        acc_one.reshape(latent_rows, heads_here, -1) * scale_one.T[:, :, None]
        + acc_two.reshape(latent_rows, heads_here, -1) * scale_two.T[:, :, None]
    )
    return (new_max, sum_one * scale_one + sum_two * scale_two, merged.reshape(latent_rows, -1))


def attend_backward(queries, grads, log_total, delta, key_heads, value_heads, valid_mask):
    latent_rows, col_count = queries.shape
    heads_here = key_heads.shape[1]
    head_size = key_heads.shape[2]
    factor = head_size ** (-0.5)
    query_heads = queries.reshape(latent_rows, heads_here, head_size)
    grad_heads = grads.reshape(latent_rows, heads_here, head_size)
    scores = (
        jnp.einsum("qhd,khd->hqk", query_heads, key_heads, preferred_element_type=jnp.float32)
        * factor
    )
    scores = jnp.where(valid_mask[None, None, :], scores, NEG)
    probs = jnp.exp(scores - log_total[:, :, None])
    dprob = jnp.einsum("qhd,khd->hqk", grad_heads, value_heads, preferred_element_type=jnp.float32)
    dscore = (probs * (dprob - delta[:, :, None]) * factor).astype(jnp.bfloat16)
    query_term = jnp.einsum("hqk,khd->qhd", dscore, key_heads, preferred_element_type=jnp.float32)
    key_term = jnp.einsum("hqk,qhd->khd", dscore, query_heads, preferred_element_type=jnp.float32)
    value_term = jnp.einsum(
        "hqk,qhd->khd", probs.astype(jnp.bfloat16), grad_heads, preferred_element_type=jnp.float32
    )
    return (
        query_term.reshape(latent_rows, col_count),
        key_term.reshape(-1, col_count),
        value_term.reshape(-1, col_count),
    )


def forward_cycle(queries, key_heads, value_heads, valid_mask):
    latent_rows, col_count = queries.shape
    heads_here = key_heads.shape[1]
    initial = (
        queries,
        jnp.full((heads_here, latent_rows), NEG, jnp.float32),
        jnp.zeros((heads_here, latent_rows), jnp.float32),
        jnp.zeros((latent_rows, col_count), jnp.float32),
    )

    def forward_cycle_step(carried, unused):
        current, row_max, row_sum, weighted = carried
        row_max, row_sum, weighted = attend_forward(
            current, row_max, row_sum, weighted, key_heads, value_heads, valid_mask
        )
        moved = shifted(current, "blk", 1)
        row_max, row_sum, weighted = shifted((row_max, row_sum, weighted), "blk", 1)
        return ((moved, row_max, row_sum, weighted), current)

    final, visited = lax.scan(forward_cycle_step, initial, None, length=lax.axis_size("blk"))
    return (final[1], final[2], final[3], visited)


def backward_cycle(visited, grad_share, log_total, delta, key_heads, value_heads, valid_mask):
    latent_rows, col_count = grad_share.shape
    token_count = key_heads.shape[0]
    initial = (
        grad_share,
        log_total,
        delta,
        jnp.zeros((latent_rows, col_count), jnp.float32),
        jnp.zeros((token_count, col_count), jnp.float32),
        jnp.zeros((token_count, col_count), jnp.float32),
    )

    def backward_cycle_step(carried, queries):
        grads, log_here, delta_here, query_grad, key_grad, value_grad = carried
        query_term, key_term, value_term = attend_backward(
            queries, grads, log_here, delta_here, key_heads, value_heads, valid_mask
        )
        moved = shifted(grads, "blk", 1)
        log_here, delta_here, query_grad = shifted(
            (log_here, delta_here, query_grad + query_term), "blk", 1
        )
        return (
            (moved, log_here, delta_here, query_grad, key_grad + key_term, value_grad + value_term),
            None,
        )

    final, unused = lax.scan(backward_cycle_step, initial, visited)
    return (final[3], final[4], final[5])


NT = (((1,), (1,)), ((), ()))
NN = (((1,), (0,)), ((), ()))
LOG2E = 1.4426950408889634


def mm(one, two, dims=NN):
    return lax.dot_general(one, two, dims, preferred_element_type=jnp.float32)


def whole(shape):
    return pl.BlockSpec(shape, lambda *unused: (0,) * len(shape))


def pairs_kernel(tok_ref, key_w_ref, value_w_ref, out_ref, *, heads):
    tok = tok_ref[...]
    keys = mm(tok, key_w_ref[...]).astype(jnp.bfloat16)
    values = mm(tok, value_w_ref[...]).astype(jnp.bfloat16)
    for h in range(heads):
        cols = slice(h * HEAD, (h + 1) * HEAD)
        out_ref[h, 0] = jnp.concatenate([keys[:, cols], values[:, cols]], axis=1)


def project_pairs(tokens, weight, groups):
    rows, width = tokens.shape
    cols = width // groups
    heads = cols // HEAD
    return pl.pallas_call(
        functools.partial(pairs_kernel, heads=heads),
        grid=(groups,),
        in_specs=[
            whole((rows, width)),
            pl.BlockSpec((width, cols), lambda n: (0, n)),
            pl.BlockSpec((width, cols), lambda n: (0, n + groups)),
        ],
        out_specs=pl.BlockSpec((heads, 1, rows, 2 * HEAD), lambda n: (0, n, 0, 0)),
        out_shape=jax.ShapeDtypeStruct((heads, groups, rows, 2 * HEAD), jnp.bfloat16),
        name="project_pairs",
    )(tokens, weight, weight)


def queries_kernel(
    index_ref, counts_ref, lat_ref, w_ref, grad_ref, out_ref, queries, *, heads, extra
):
    step = pl.program_id(0)
    rows = grad_ref.shape[0]

    @pl.when(step == 0)
    def _():
        queries[...] = mm(lat_ref[...], w_ref[...]).astype(jnp.bfloat16)

    lane = lax.broadcasted_iota(jnp.int32, (extra, 2 * HEAD), 1)
    counts = jnp.zeros((extra, 2 * HEAD), jnp.float32)
    for n in range(counts_ref.shape[0]):
        counts = jnp.where(lane == n, counts_ref[n].astype(jnp.float32), counts)
    out_ref[0, rows:, :] = counts.astype(jnp.bfloat16)
    for h in range(heads):
        cols = slice(h * HEAD, (h + 1) * HEAD)

        @pl.when(step == h)
        def _(cols=cols):
            out_ref[0, :rows, :] = jnp.concatenate([queries[:, cols], grad_ref[:, cols]], axis=1)


def project_queries(latents, weight, cotangent, index, counts, groups, extra=16):
    rows, width = latents.shape
    cols = width // groups
    heads = cols // HEAD
    return pl.pallas_call(
        functools.partial(queries_kernel, heads=heads, extra=extra),
        grid_spec=pltpu.PrefetchScalarGridSpec(
            num_scalar_prefetch=2,
            grid=(heads,),
            in_specs=[
                pl.BlockSpec((rows, width), lambda i, at, c: (0, 0)),
                pl.BlockSpec((width, cols), lambda i, at, c: (0, at[0])),
                pl.BlockSpec((rows, cols), lambda i, at, c: (0, at[0])),
            ],
            out_specs=pl.BlockSpec(
                (1, rows + extra, 2 * HEAD), lambda i, at, c: (i ^ at[1], 0, 0)
            ),
            scratch_shapes=[pltpu.VMEM((rows, cols), jnp.bfloat16)],
        ),
        out_shape=jax.ShapeDtypeStruct((heads, rows + extra, 2 * HEAD), jnp.bfloat16),
        name="project_queries",
    )(index, counts, latents, weight, cotangent)


def count_of(counts_ref, index_ref, source):
    return counts_ref[source // 4 ^ index_ref[1], source % 4]


def pack_tokens(counts_ref, index_ref, kv_ref, wide, kv, kvt, valid, tile):
    sources, slot, width = kv_ref.shape
    padded = kv.shape[0]
    at = 0
    for s in range(sources):
        wide[pl.ds(at, slot), :] = kv_ref[s].astype(jnp.float32)
        at = at + count_of(counts_ref, index_ref, s)
    for t in range(0, padded, tile):
        size = min(tile, padded - t)
        part = wide[t:t + size, :]
        if t + size > valid:
            part = jnp.where(
                lax.broadcasted_iota(jnp.int32, (size, width), 0) < valid - t, part, wide[:1, :]
            )
        kv[t:t + size, :] = part.astype(jnp.bfloat16)
        kvt[:, t:t + size] = part.T.astype(jnp.bfloat16)


def unpack_tokens(counts_ref, index_ref, acc, wide, dkv_ref, tile):
    sources, slot, width = dkv_ref.shape
    padded = acc.shape[1]
    scale = jnp.where(
        lax.broadcasted_iota(jnp.int32, (tile, width), 1) < HEAD, HEAD ** (-0.5), 1.0
    )
    for t in range(0, padded, tile):
        size = min(tile, padded - t)
        wide[t:t + size, :] = acc[:, t:t + size].T * scale[:size]
    row = lax.broadcasted_iota(jnp.int32, (slot, width), 0)
    at = 0
    for s in range(sources):
        count = count_of(counts_ref, index_ref, s)
        rows = wide[pl.ds(at, slot), :]
        dkv_ref[s] = jnp.where(row < count, rows, 0.0).astype(jnp.bfloat16)
        at = at + count


class Block:
    def __init__(self, qg, slot, kv, kvt, acc, scores, dprobs, sums, valid):
        self.slot, self.kv, self.kvt, self.acc, self.valid = slot, kv, kvt, acc, valid
        self.scores, self.dprobs, self.sums = scores.at[slot], dprobs.at[slot], sums.at[slot]
        self.count, width = qg.shape
        lane = lax.broadcasted_iota(jnp.int32, (self.count, width), 1)
        zero = jnp.zeros_like(qg)
        self.query = jnp.where(lane < HEAD, qg, zero)
        self.grad = jnp.where(lane < HEAD, zero, qg)
        turned = qg.astype(jnp.float32).T
        self.grad_wide = turned[HEAD:, :]
        self.query_t = turned[:HEAD, :].astype(jnp.bfloat16)
        self.grad_t = turned[HEAD:, :].astype(jnp.bfloat16)

    def fold(self, part, op):
        return op(part.reshape(part.shape[0] // 8, 8, self.count), axis=0)

    def score(self, rows, highest):
        part = mm(self.kv[rows, :], self.query, NT)
        self.scores[rows, :] = part
        self.dprobs[rows, :] = mm(self.kv[rows, :], self.grad, NT)
        return jnp.maximum(highest, self.fold(part, jnp.max))

    def scored(self, highest):
        padded = self.kv.shape[0]
        self.top = jnp.max(highest, axis=0, keepdims=True)
        self.scores[self.valid:, :] = jnp.full((padded - self.valid, self.count), NEG, jnp.float32)
        self.sums[...] = jnp.zeros(self.sums.shape, jnp.float32)

    def attend(self, rows, total):
        power = jnp.exp2((self.scores[rows, :] - self.top) * (HEAD ** (-0.5) * LOG2E))
        self.scores[rows, :] = power
        self.sums[:HEAD, :] += mm(self.kvt[HEAD:, rows], power.astype(jnp.bfloat16))
        return total + self.fold(power, jnp.sum)

    def attended(self, total):
        self.inverse = 1.0 / jnp.sum(total, axis=0, keepdims=True)
        self.out = self.sums[:HEAD, :] * self.inverse
        self.delta = jnp.sum(self.grad_wide * self.out, axis=0, keepdims=True)

    def back(self, rows, unused):
        prob = self.scores[rows, :] * self.inverse
        dscore = (prob * (self.dprobs[rows, :] - self.delta)).astype(jnp.bfloat16)
        self.acc[:HEAD, rows] += mm(self.query_t, dscore, NT)
        self.acc[HEAD:, rows] += mm(self.grad_t, prob.astype(jnp.bfloat16), NT)
        self.sums[HEAD:, :] += mm(self.kvt[:HEAD, rows], dscore)
        return unused

    def ended(self, unused):
        both = jnp.concatenate([self.out, self.sums[HEAD:, :] * HEAD ** (-0.5)], axis=0)
        self.both = both.T.astype(jnp.bfloat16)


def attend_blocks(qgs, scores, dprobs, sums, kv, kvt, acc, valid, tile):
    count = len(qgs)
    padded = kv.shape[0]
    blocks = []
    for step in range(count + 2):
        if step < count:
            blocks.append(
                Block(qgs[step], step % 3, kv, kvt, acc, scores, dprobs, sums, valid)
            )
        work = []
        if 0 <= step - 2 < count:
            work.append((blocks[step - 2].back, blocks[step - 2].ended, 0.0))
        if 0 <= step - 1 < count:
            work.append((blocks[step - 1].attend, blocks[step - 1].attended, 0.0))
        if step < count:
            work.append((blocks[step].score, blocks[step].scored, NEG))

        def body(k, carried, work=work):
            rows = pl.ds(pl.multiple_of(k * tile, tile), tile)
            return tuple(one[0](rows, held) for one, held in zip(work, carried))

        found = lax.fori_loop(
            0,
            padded // tile,
            body,
            tuple(jnp.full((8, block_rows(qgs)), one[2], jnp.float32) for one in work),
        )
        for one, held in zip(work, found):
            one[1](held)
    return [block.both for block in blocks]


def block_rows(qgs):
    return qgs[0].shape[0]


def first_kernel(
    counts_ref, index_ref, kv_ref, qg_ref, *refs, valid, tile
):
    pair = qg_ref.shape[0]
    outs, (kv, kvt, acc, wide, scores, dprobs, sums) = refs[:-7], refs[-7:]

    @pl.when(pl.program_id(0) == 0)
    def _():
        pack_tokens(counts_ref, index_ref, kv_ref, wide, kv, kvt, valid, tile)
        acc[...] = jnp.zeros(acc.shape, jnp.float32)

    found = attend_blocks(
        [qg_ref[k] for k in range(pair)], scores, dprobs, sums, kv, kvt, acc, valid, tile
    )
    for k in range(pair):
        outs[0][k] = found[k]
        outs[1 + k][...] = found[k]


def later_kernel(counts_ref, index_ref, kv, kvt, acc_ref, qg_ref, *refs, valid, tile):
    *outs, out_ref, acc, wide, scores, dprobs, sums = refs

    @pl.when(pl.program_id(0) == 0)
    def _():
        acc[...] = acc_ref[...]

    pair = qg_ref.shape[0]
    found = attend_blocks(
        [qg_ref[k] for k in range(pair)], scores, dprobs, sums, kv, kvt, acc, valid, tile
    )
    for k in range(pair):
        outs[0][k] = found[k]
        outs[1 + k][...] = found[k]

    @pl.when(pl.program_id(0) == pl.num_programs(0) - 1)
    def _():
        unpack_tokens(counts_ref, index_ref, acc, wide, out_ref, tile)


def attention_first(counts, index, kv, qg, valid, block, tile=1280):
    sources, slot, width = kv.shape
    blocks = qg.shape[0]
    padded = -(-valid // 128) * 128
    room = padded + slot + 16
    shapes = [
        jax.ShapeDtypeStruct((padded, width), jnp.bfloat16),
        jax.ShapeDtypeStruct((width, padded), jnp.bfloat16),
        jax.ShapeDtypeStruct((width, padded), jnp.float32),
    ]
    out_shape = jax.ShapeDtypeStruct((blocks, block, width), jnp.bfloat16)
    pair = blocks
    out_spec = pl.BlockSpec((pair, block, width), lambda i, c, at: (i, 0, 0))
    alone = [jax.ShapeDtypeStruct((block, width), jnp.bfloat16)] * blocks
    return pl.pallas_call(
        functools.partial(first_kernel, valid=valid, tile=tile),
        grid_spec=pltpu.PrefetchScalarGridSpec(
            num_scalar_prefetch=2,
            grid=(blocks // pair,),
            in_specs=[
                whole(kv.shape),
                pl.BlockSpec((pair, block, width), lambda i, c, at: (i, 0, 0)),
            ],
            out_specs=[out_spec] + [whole(s.shape) for s in alone + shapes],
            scratch_shapes=[
                pltpu.VMEM((room, width), jnp.float32),
                pltpu.VMEM((3, padded, block), jnp.float32),
                pltpu.VMEM((3, padded, block), jnp.float32),
                pltpu.VMEM((3, width, block), jnp.float32),
            ],
        ),
        out_shape=[out_shape] + alone + shapes,
        cost_estimate=attention_cost(blocks * block, padded),
        name="attention_first",
    )(counts, index, kv, qg)


def attention_later(counts, index, packed, kv_shape, qg, valid, at, block, tile=1280):
    blocks, _, width = qg.shape
    padded, pair = packed[0].shape[0], blocks
    out_shape = [
        jax.ShapeDtypeStruct((blocks, block, width), jnp.bfloat16),
        *[jax.ShapeDtypeStruct((block, width), jnp.bfloat16)] * blocks,
        jax.ShapeDtypeStruct(kv_shape, jnp.bfloat16),
    ]
    return pl.pallas_call(
        functools.partial(later_kernel, valid=valid, tile=tile),
        grid_spec=pltpu.PrefetchScalarGridSpec(
            num_scalar_prefetch=2,
            grid=(blocks // pair,),
            in_specs=[whole(part.shape) for part in packed]
            + [pl.BlockSpec((pair, block, width), lambda i, c, b: (i, at, 0))],
            out_specs=[
                pl.BlockSpec((pair, block, width), lambda i, c, b: (i, 0, 0)),
                *[whole((block, width))] * blocks,
                whole(kv_shape),
            ],
            scratch_shapes=[
                pltpu.VMEM(packed[2].shape, jnp.float32),
                pltpu.VMEM((padded + kv_shape[1] + 16, width), jnp.float32),
                pltpu.VMEM((3, padded, block), jnp.float32),
                pltpu.VMEM((3, padded, block), jnp.float32),
                pltpu.VMEM((3, width, block), jnp.float32),
            ],
        ),
        out_shape=out_shape,
        cost_estimate=attention_cost(blocks * block, padded),
        name="attention_later",
    )(counts, index, *packed, qg)


def attention_cost(rows, padded):
    return pl.CostEstimate(
        flops=24 * rows * padded * 256,
        transcendentals=rows * padded,
        bytes_accessed=8 * padded * 2 * HEAD,
    )


def side_by_side(part, heads, first):
    lanes = slice(0, HEAD) if first else slice(HEAD, 2 * HEAD)
    return jnp.concatenate([part[h][:, lanes] for h in range(heads)], axis=1)


def token_grad_kernel(dkv_ref, key_w_ref, value_w_ref, out_ref, acc, *, heads):
    step = pl.program_id(0)

    @pl.when(step == 0)
    def _():
        acc[...] = jnp.zeros(acc.shape, jnp.float32)

    part = [dkv_ref[h, 0] for h in range(heads)]
    keys = side_by_side(part, heads, True)
    values = side_by_side(part, heads, False)
    acc[...] += mm(keys, key_w_ref[...], NT) + mm(values, value_w_ref[...], NT)

    @pl.when(step == pl.num_programs(0) - 1)
    def _():
        out_ref[...] = acc[...].astype(jnp.bfloat16)


def token_grad(dkv, weight):
    heads, groups, rows, pair = dkv.shape
    width = weight.shape[0]
    cols = heads * HEAD
    return pl.pallas_call(
        functools.partial(token_grad_kernel, heads=heads),
        grid=(groups,),
        in_specs=[
            pl.BlockSpec((heads, 1, rows, pair), lambda n: (0, n, 0, 0)),
            pl.BlockSpec((width, cols), lambda n: (0, n)),
            pl.BlockSpec((width, cols), lambda n: (0, n + groups)),
        ],
        out_specs=whole((rows, width)),
        out_shape=jax.ShapeDtypeStruct((rows, width), jnp.bfloat16),
        scratch_shapes=[pltpu.VMEM((rows, width), jnp.float32)],
        name="token_grad",
    )(dkv, weight, weight)


def latent_grad_kernel(index_ref, *refs, heads, groups, split):
    w_ref = refs[groups * heads if split else groups]
    out_ref, grad_ref = refs[-2:]
    cols = heads * HEAD
    total = None
    for k in range(groups):
        if split:
            part = [refs[k * heads + h][...] for h in range(heads)]
            part = [chosen(part, h, index_ref[1]) for h in range(heads)]
        else:
            part = [refs[k][h ^ index_ref[1]] for h in range(heads)]
        at = pl.multiple_of((index_ref[0] ^ k) * cols, cols)
        out_ref[:, pl.ds(at, cols)] = side_by_side(part, heads, True)
        term = mm(side_by_side(part, heads, False), w_ref[:, pl.ds(at, cols)], NT)
        total = term if total is None else total + term
    grad_ref[...] = total.astype(jnp.bfloat16)


def chosen(part, h, flip):
    low = jnp.where(flip % 2 == 1, part[h ^ 1], part[h])
    high = jnp.where(flip % 2 == 1, part[h ^ 3], part[h ^ 2])
    return jnp.where(flip // 2 == 1, high, low)


def latent_grad(index, parts, weight, chunk, chunks, earlier):
    split = isinstance(parts[0], list)
    groups = len(parts)
    heads = len(parts[0]) if split else parts[0].shape[0]
    parts = sum(parts, []) if split else parts
    rows = parts[0].shape[-2]
    width = weight.shape[0]
    shape = jax.ShapeDtypeStruct((rows * chunks, width), jnp.bfloat16)
    out_spec = pl.BlockSpec((rows, width), lambda i, at: (chunk, 0))
    return pl.pallas_call(
        functools.partial(latent_grad_kernel, heads=heads, groups=groups, split=split),
        grid_spec=pltpu.PrefetchScalarGridSpec(
            num_scalar_prefetch=1,
            grid=(1,),
            in_specs=[
                pl.BlockSpec(part.shape, lambda i, at, n=part.ndim: (0,) * n) for part in parts
            ]
            + [pl.BlockSpec(weight.shape, lambda i, at: (0, 0))]
            + [pl.BlockSpec(memory_space=pl.ANY)] * len(earlier),
            out_specs=[out_spec, out_spec],
        ),
        out_shape=[shape, shape],
        input_output_aliases={2 + len(parts) + k: k for k in range(len(earlier))},
        name="latent_grad",
    )(index, *parts, weight, *earlier)


def weight_grad_kernel(*refs, slots):
    out_ref, one_ref, two_ref = refs[-1], refs[slots], refs[slots + 1]
    rows = two_ref.shape[1]
    total = None
    for k in range(slots):
        low = one_ref[k].astype(jnp.float32).T[HEAD:, :].astype(jnp.bfloat16)
        term = mm(low, refs[k][:rows, :])
        total = term if total is None else total + term
        low = two_ref[k].astype(jnp.float32).T[HEAD:, :].astype(jnp.bfloat16)
        total = total + mm(low, refs[k][rows:, :])
    out_ref[...] = total.astype(jnp.bfloat16)


def weight_grad(latents, one, two):
    return pl.pallas_call(
        functools.partial(weight_grad_kernel, slots=len(latents)),
        out_shape=jax.ShapeDtypeStruct((HEAD, latents[0].shape[1]), jnp.bfloat16),
        name="weight_grad",
    )(*latents, one, two)


def turn_kernel(index_ref, *refs):
    out_ref, scratch = refs[-2:]
    for k, ref in enumerate(refs[:-2]):
        at = pl.multiple_of((index_ref[1] ^ k) * HEAD, HEAD)
        scratch[pl.ds(at, HEAD), :] = ref[...].astype(jnp.float32)
    out_ref[...] = scratch[...].T.astype(jnp.bfloat16)


def turn(index, parts):
    width = parts[0].shape[1]
    cols = HEAD * len(parts)
    spec = pl.BlockSpec((HEAD, width), lambda i, at: (0, 0))
    return pl.pallas_call(
        turn_kernel,
        grid_spec=pltpu.PrefetchScalarGridSpec(
            num_scalar_prefetch=1,
            grid=(1,),
            in_specs=[spec] * len(parts),
            out_specs=pl.BlockSpec((width, cols), lambda i, at: (0, 0)),
            scratch_shapes=[pltpu.VMEM((cols, width), jnp.float32)],
        ),
        out_shape=jax.ShapeDtypeStruct((width, cols), jnp.bfloat16),
        name="turn",
    )(index, *parts)


def swapped(shard, axis, bit):
    return lax.ppermute(shard, axis, [(i, i ^ bit) for i in range(lax.axis_size(axis))])


def exchanged(slots, axis):
    return [slots[0]] + [
        swapped(slots[k], axis, k) for k in range(1, lax.axis_size(axis))
    ]


def gathered(shard, axis):
    near = swapped(shard, axis, 1)
    far = swapped(shard, axis, 2)
    return [shard, near, far, swapped(far, axis, 1)]


def by_head(tokens, latents, cotangent, query_weight, keyvalue_weight, counts):
    blocks = lax.axis_size("blk")
    groups = lax.axis_size("narrow")
    everyone = ("blk", "narrow")
    tok_rows, width = tokens.shape
    latent_rows = latents.shape[0]
    chunks = 2
    valid = tok_rows * groups * 614 // 1024 * blocks
    index = jnp.stack([lax.axis_index("narrow"), lax.axis_index("blk")]).astype(jnp.int32)
    pairs = project_pairs(tokens, keyvalue_weight, groups)
    pairs = pairs.reshape(blocks * groups, tok_rows, 2 * HEAD)
    held, pairs = lax.optimization_barrier((latents, pairs))
    pairs = lax.all_to_all(pairs, everyone, 0, 0, tiled=True)
    qg = project_queries(held, query_weight, cotangent, index, counts.reshape(groups), groups)
    qg = jnp.stack(exchanged(qg, "blk"))
    all_counts = qg[:, latent_rows, :groups].astype(jnp.int32)
    half = latent_rows // chunks
    held, qg = lax.optimization_barrier((latents, qg))
    far = swapped(held, "blk", 2)
    found = attention_first(all_counts, index, pairs, qg, valid, half)
    one, ones, packed = found[0], found[1:1 + blocks], found[1 + blocks:]
    near_one, far_one = swapped(one, "narrow", 1), swapped(one, "narrow", 2)
    two, *twos, dkv = attention_later(
        all_counts, index, packed, pairs.shape, qg, valid, 1, half
    )
    dkv, ones, twos, near_one, far_one, far = lax.optimization_barrier(
        (dkv, ones, twos, near_one, far_one, far)
    )
    every = [latents, swapped(latents, "blk", 1), far, swapped(far, "blk", 1)]
    last_one = swapped(far_one, "narrow", 1)
    dkv = lax.all_to_all(dkv, everyone, 0, 0, tiled=True)
    own_two = jnp.stack(exchanged(twos, "blk"))
    own_two, every, two = lax.optimization_barrier((own_two, every, two))
    part_two = gathered(own_two, "narrow")
    part_one = [exchanged(held, "blk") for held in (ones, near_one, far_one, last_one)]
    grad_query_weight = turn(index, gathered(weight_grad(every, one, two), "blk"))
    grad_tokens = token_grad(
        dkv.reshape(blocks, groups, tok_rows, 2 * HEAD), keyvalue_weight
    )
    done = latent_grad(index, part_one, query_weight, 0, chunks, ())
    done, part_two = lax.optimization_barrier((done, part_two))
    latent_out, grad_latents = latent_grad(index, part_two, query_weight, 1, chunks, done)
    return (latent_out, grad_latents, grad_query_weight, grad_tokens)


def on_device(tokens, latents, cotangent, query_weight, keyvalue_weight, counts):
    narrow_size = lax.axis_size("narrow")
    narrow_index = lax.axis_index("narrow")
    tok_rows = tokens.shape[0]
    model_width = tokens.shape[1]
    share = model_width // narrow_size
    queries = jnp.dot(latents, query_weight, preferred_element_type=jnp.float32).astype(
        jnp.bfloat16
    )
    pairs = jnp.dot(tokens, keyvalue_weight, preferred_element_type=jnp.float32).astype(
        jnp.bfloat16
    )
    key_heads = pairs[:, :model_width].reshape(tok_rows, HEADS, HEAD)
    value_heads = pairs[:, model_width:].reshape(tok_rows, HEADS, HEAD)
    valid_mask = jnp.arange(tok_rows) < counts[0, narrow_index]
    row_max, row_sum, weighted, visited = forward_cycle(queries, key_heads, value_heads, valid_mask)
    row_max, row_sum, weighted = merged_2((row_max, row_sum, weighted), "narrow", join_partials)
    heads_here = row_max.shape[0]
    latent_rows = weighted.shape[0]
    attended = weighted.reshape(latent_rows, heads_here, HEAD) / row_sum.T[:, :, None]
    attended_low = attended.reshape(latent_rows, -1).astype(jnp.bfloat16)
    delta = jnp.sum(
        cotangent.astype(jnp.float32).reshape(latent_rows, heads_here, HEAD) * attended, axis=2
    ).T
    log_total = row_max + jnp.log(row_sum)
    query_grad, key_grad, value_grad = backward_cycle(
        visited, cotangent, log_total, delta, key_heads, value_heads, valid_mask
    )
    pair_grad = jnp.concatenate([key_grad, value_grad], axis=1).astype(jnp.bfloat16)
    query_part = lax.psum_scatter(query_grad, "narrow", scatter_dimension=1, tiled=True)
    query_low = query_part.astype(jnp.bfloat16)
    weight_cols = lax.dynamic_slice_in_dim(query_weight, narrow_index * share, share, 1)
    weight_term = lax.dot_general(
        latents, query_low, (((0,), (0,)), ((), ())), preferred_element_type=jnp.float32
    )
    grad_query_weight = lax.psum(weight_term, "blk").astype(jnp.bfloat16)
    latent_term = lax.dot_general(
        query_low, weight_cols, (((1,), (1,)), ((), ())), preferred_element_type=jnp.float32
    )
    grad_latents = lax.psum(latent_term, "narrow").astype(jnp.bfloat16)
    grad_tokens = lax.dot_general(
        pair_grad, keyvalue_weight, (((1,), (1,)), ((), ())), preferred_element_type=jnp.float32
    ).astype(jnp.bfloat16)
    return (attended_low, grad_latents, grad_query_weight, grad_tokens)


def solution(mesh):
    placed = (
        P(("groups", "blk", "narrow"), None),
        P("blk", None),
        P(("groups", "blk"), None),
        P(),
        P(),
        P(("groups", "blk"), None),
    )
    one_head_each = mesh.shape["blk"] == 4 and mesh.shape["narrow"] == 4
    return jax.shard_map(
        by_head if one_head_each else on_device,
        mesh=mesh,
        in_specs=placed,
        out_specs=(
            P(("groups", "blk"), None),
            P(("groups", "blk"), None),
            P("groups", "narrow"),
            P(("groups", "blk", "narrow"), None),
        ),
        check_vma=False,
    )
```

```python
import functools

import jax
import jax.numpy as jnp
from jax import lax
from jax.experimental import pallas as pl
from jax.experimental.pallas import tpu as pltpu
from jax.sharding import PartitionSpec as P

HEADS = 16
HEAD = 64


NEG = -1e30


def shifted(shard, axis, by):
    length = lax.axis_size(axis)
    return lax.ppermute(shard, axis, [(i, (i + by) % length) for i in range(length)])


def merged_2(shard, axis, combine):
    everything = jax.tree.map(lambda part: lax.all_gather(part, axis), shard)
    initial = jax.tree.map(lambda part: part[0], everything)

    def turn(k, so_far):
        return combine(so_far, jax.tree.map(lambda part: part[k], everything))

    return lax.fori_loop(1, lax.axis_size(axis), turn, initial)


def attend_forward(queries, row_max, row_sum, weighted, key_heads, value_heads, valid_mask):
    latent_rows, col_count = queries.shape
    heads_here = key_heads.shape[1]
    head_size = key_heads.shape[2]
    query_heads = queries.reshape(latent_rows, heads_here, head_size)
    scores = jnp.einsum(
        "qhd,khd->hqk", query_heads, key_heads, preferred_element_type=jnp.float32
    ) * head_size ** (-0.5)
    scores = jnp.where(valid_mask[None, None, :], scores, NEG)
    new_max = jnp.maximum(row_max, jnp.max(scores, axis=2))
    powers = jnp.exp(scores - new_max[:, :, None])
    rescale = jnp.exp(row_max - new_max)
    row_sum = row_sum * rescale + jnp.sum(powers, axis=2)
    update = jnp.einsum(
        "hqk,khd->qhd", powers.astype(jnp.bfloat16), value_heads, preferred_element_type=jnp.float32
    )
    weighted = weighted.reshape(latent_rows, heads_here, head_size) * rescale.T[:, :, None] + update
    return (new_max, row_sum, weighted.reshape(latent_rows, col_count))


def join_partials(earlier, latter):
    max_one, sum_one, acc_one = earlier
    max_two, sum_two, acc_two = latter
    new_max = jnp.maximum(max_one, max_two)
    scale_one = jnp.exp(max_one - new_max)
    scale_two = jnp.exp(max_two - new_max)
    latent_rows = acc_one.shape[0]
    heads_here = max_one.shape[0]
    merged = (
        acc_one.reshape(latent_rows, heads_here, -1) * scale_one.T[:, :, None]
        + acc_two.reshape(latent_rows, heads_here, -1) * scale_two.T[:, :, None]
    )
    return (new_max, sum_one * scale_one + sum_two * scale_two, merged.reshape(latent_rows, -1))


def attend_backward(queries, grads, log_total, delta, key_heads, value_heads, valid_mask):
    latent_rows, col_count = queries.shape
    heads_here = key_heads.shape[1]
    head_size = key_heads.shape[2]
    factor = head_size ** (-0.5)
    query_heads = queries.reshape(latent_rows, heads_here, head_size)
    grad_heads = grads.reshape(latent_rows, heads_here, head_size)
    scores = (
        jnp.einsum("qhd,khd->hqk", query_heads, key_heads, preferred_element_type=jnp.float32)
        * factor
    )
    scores = jnp.where(valid_mask[None, None, :], scores, NEG)
    probs = jnp.exp(scores - log_total[:, :, None])
    dprob = jnp.einsum("qhd,khd->hqk", grad_heads, value_heads, preferred_element_type=jnp.float32)
    dscore = (probs * (dprob - delta[:, :, None]) * factor).astype(jnp.bfloat16)
    query_term = jnp.einsum("hqk,khd->qhd", dscore, key_heads, preferred_element_type=jnp.float32)
    key_term = jnp.einsum("hqk,qhd->khd", dscore, query_heads, preferred_element_type=jnp.float32)
    value_term = jnp.einsum(
        "hqk,qhd->khd", probs.astype(jnp.bfloat16), grad_heads, preferred_element_type=jnp.float32
    )
    return (
        query_term.reshape(latent_rows, col_count),
        key_term.reshape(-1, col_count),
        value_term.reshape(-1, col_count),
    )


def forward_cycle(queries, key_heads, value_heads, valid_mask):
    latent_rows, col_count = queries.shape
    heads_here = key_heads.shape[1]
    initial = (
        queries,
        jnp.full((heads_here, latent_rows), NEG, jnp.float32),
        jnp.zeros((heads_here, latent_rows), jnp.float32),
        jnp.zeros((latent_rows, col_count), jnp.float32),
    )

    def forward_cycle_step(carried, unused):
        current, row_max, row_sum, weighted = carried
        row_max, row_sum, weighted = attend_forward(
            current, row_max, row_sum, weighted, key_heads, value_heads, valid_mask
        )
        moved = shifted(current, "blk", 1)
        row_max, row_sum, weighted = shifted((row_max, row_sum, weighted), "blk", 1)
        return ((moved, row_max, row_sum, weighted), current)

    final, visited = lax.scan(forward_cycle_step, initial, None, length=lax.axis_size("blk"))
    return (final[1], final[2], final[3], visited)


def backward_cycle(visited, grad_share, log_total, delta, key_heads, value_heads, valid_mask):
    latent_rows, col_count = grad_share.shape
    token_count = key_heads.shape[0]
    initial = (
        grad_share,
        log_total,
        delta,
        jnp.zeros((latent_rows, col_count), jnp.float32),
        jnp.zeros((token_count, col_count), jnp.float32),
        jnp.zeros((token_count, col_count), jnp.float32),
    )

    def backward_cycle_step(carried, queries):
        grads, log_here, delta_here, query_grad, key_grad, value_grad = carried
        query_term, key_term, value_term = attend_backward(
            queries, grads, log_here, delta_here, key_heads, value_heads, valid_mask
        )
        moved = shifted(grads, "blk", 1)
        log_here, delta_here, query_grad = shifted(
            (log_here, delta_here, query_grad + query_term), "blk", 1
        )
        return (
            (moved, log_here, delta_here, query_grad, key_grad + key_term, value_grad + value_term),
            None,
        )

    final, unused = lax.scan(backward_cycle_step, initial, visited)
    return (final[3], final[4], final[5])


NT = (((1,), (1,)), ((), ()))
NN = (((1,), (0,)), ((), ()))
LOG2E = 1.4426950408889634


def mm(one, two, dims=NN):
    return lax.dot_general(one, two, dims, preferred_element_type=jnp.float32)


def whole(shape):
    return pl.BlockSpec(shape, lambda *unused: (0,) * len(shape))


def in_vmem(array):
    return pltpu.with_memory_space_constraint(array, pltpu.VMEM)


def held_whole():
    return pl.BlockSpec(memory_space=pltpu.VMEM)


def pairs_kernel(tok_ref, key_w_ref, value_w_ref, out_ref, *, heads):
    tok = tok_ref[...]
    keys = mm(tok, key_w_ref[...]).astype(jnp.bfloat16)
    values = mm(tok, value_w_ref[...]).astype(jnp.bfloat16)
    for h in range(heads):
        cols = slice(h * HEAD, (h + 1) * HEAD)
        out_ref[h, 0] = jnp.concatenate([keys[:, cols], values[:, cols]], axis=1)


def project_pairs(tokens, weight, groups):
    rows, width = tokens.shape
    cols = width // groups
    heads = cols // HEAD
    return pl.pallas_call(
        functools.partial(pairs_kernel, heads=heads),
        grid=(groups,),
        in_specs=[
            whole((rows, width)),
            pl.BlockSpec((width, cols), lambda n: (0, n)),
            pl.BlockSpec((width, cols), lambda n: (0, n + groups)),
        ],
        out_specs=pl.BlockSpec((heads, 1, rows, 2 * HEAD), lambda n: (0, n, 0, 0)),
        out_shape=jax.ShapeDtypeStruct((heads, groups, rows, 2 * HEAD), jnp.bfloat16),
        name="project_pairs",
    )(tokens, weight, weight)


def queries_kernel(
    index_ref, counts_ref, lat_ref, w_ref, grad_ref, out_ref, queries, *, heads, extra
):
    step = pl.program_id(0)
    rows = grad_ref.shape[0]

    @pl.when(step == 0)
    def _():
        queries[...] = mm(lat_ref[...], w_ref[...]).astype(jnp.bfloat16)

    lane = lax.broadcasted_iota(jnp.int32, (extra, 2 * HEAD), 1)
    counts = jnp.zeros((extra, 2 * HEAD), jnp.float32)
    for n in range(counts_ref.shape[0]):
        counts = jnp.where(lane == n, counts_ref[n].astype(jnp.float32), counts)
    out_ref[0, rows:, :] = counts.astype(jnp.bfloat16)
    for h in range(heads):
        cols = slice(h * HEAD, (h + 1) * HEAD)

        @pl.when(step == h)
        def _(cols=cols):
            out_ref[0, :rows, :] = jnp.concatenate([queries[:, cols], grad_ref[:, cols]], axis=1)


def project_queries(latents, weight, cotangent, index, counts, groups, extra=16):
    rows, width = latents.shape
    cols = width // groups
    heads = cols // HEAD
    return pl.pallas_call(
        functools.partial(queries_kernel, heads=heads, extra=extra),
        grid_spec=pltpu.PrefetchScalarGridSpec(
            num_scalar_prefetch=2,
            grid=(heads,),
            in_specs=[
                pl.BlockSpec((rows, width), lambda i, at, c: (0, 0)),
                pl.BlockSpec((width, cols), lambda i, at, c: (0, at[0])),
                pl.BlockSpec((rows, cols), lambda i, at, c: (0, at[0])),
            ],
            out_specs=pl.BlockSpec(
                (1, rows + extra, 2 * HEAD), lambda i, at, c: (i ^ at[1], 0, 0)
            ),
            scratch_shapes=[pltpu.VMEM((rows, cols), jnp.bfloat16)],
        ),
        out_shape=jax.ShapeDtypeStruct((heads, rows + extra, 2 * HEAD), jnp.bfloat16),
        name="project_queries",
    )(index, counts, latents, weight, cotangent)


def count_of(counts_ref, index_ref, source):
    return counts_ref[source // 4 ^ index_ref[1], source % 4]


def pack_tokens(counts_ref, index_ref, kv_ref, wide, kv, kvt, valid, tile):
    sources, slot, width = kv_ref.shape
    padded = kv.shape[0]
    at = 0
    for s in range(sources):
        wide[pl.ds(at, slot), :] = kv_ref[s].astype(jnp.float32)
        at = at + count_of(counts_ref, index_ref, s)
    for t in range(0, padded, tile):
        size = min(tile, padded - t)
        part = wide[t:t + size, :]
        if t + size > valid:
            part = jnp.where(
                lax.broadcasted_iota(jnp.int32, (size, width), 0) < valid - t, part, wide[:1, :]
            )
        kv[t:t + size, :] = part.astype(jnp.bfloat16)
        kvt[:, t:t + size] = part.T.astype(jnp.bfloat16)


def unpack_tokens(counts_ref, index_ref, acc, wide, dkv_ref, tile):
    sources, slot, width = dkv_ref.shape
    padded = acc.shape[1]
    scale = jnp.where(
        lax.broadcasted_iota(jnp.int32, (tile, width), 1) < HEAD, HEAD ** (-0.5), 1.0
    )
    for t in range(0, padded, tile):
        size = min(tile, padded - t)
        wide[t:t + size, :] = acc[:, t:t + size].T * scale[:size]
    row = lax.broadcasted_iota(jnp.int32, (slot, width), 0)
    at = 0
    for s in range(sources):
        count = count_of(counts_ref, index_ref, s)
        rows = wide[pl.ds(at, slot), :]
        dkv_ref[s] = jnp.where(row < count, rows, 0.0).astype(jnp.bfloat16)
        at = at + count


class Block:
    def __init__(self, qg, slot, kv, kvt, acc, scores, dprobs, sums, valid):
        self.slot, self.kv, self.kvt, self.acc, self.valid = slot, kv, kvt, acc, valid
        self.scores, self.dprobs, self.sums = scores.at[slot], dprobs.at[slot], sums.at[slot]
        self.count, width = qg.shape
        lane = lax.broadcasted_iota(jnp.int32, (self.count, width), 1)
        zero = jnp.zeros_like(qg)
        self.query = jnp.where(lane < HEAD, qg, zero)
        self.grad = jnp.where(lane < HEAD, zero, qg)
        turned = qg.astype(jnp.float32).T
        self.grad_wide = turned[HEAD:, :]
        self.query_t = turned[:HEAD, :].astype(jnp.bfloat16)
        self.grad_t = turned[HEAD:, :].astype(jnp.bfloat16)

    def fold(self, part, op):
        return op(part.reshape(part.shape[0] // 8, 8, self.count), axis=0)

    def score(self, rows, highest):
        part = mm(self.kv[rows, :], self.query, NT)
        self.scores[rows, :] = part
        self.dprobs[rows, :] = mm(self.kv[rows, :], self.grad, NT)
        return jnp.maximum(highest, self.fold(part, jnp.max))

    def scored(self, highest):
        padded = self.kv.shape[0]
        self.top = jnp.max(highest, axis=0, keepdims=True)
        self.scores[self.valid:, :] = jnp.full((padded - self.valid, self.count), NEG, jnp.float32)
        self.sums[...] = jnp.zeros(self.sums.shape, jnp.float32)

    def attend(self, rows, total):
        power = jnp.exp2((self.scores[rows, :] - self.top) * (HEAD ** (-0.5) * LOG2E))
        self.scores[rows, :] = power
        self.sums[:HEAD, :] += mm(self.kvt[HEAD:, rows], power.astype(jnp.bfloat16))
        return total + self.fold(power, jnp.sum)

    def attended(self, total):
        self.inverse = 1.0 / jnp.sum(total, axis=0, keepdims=True)
        self.out = self.sums[:HEAD, :] * self.inverse
        self.delta = jnp.sum(self.grad_wide * self.out, axis=0, keepdims=True)

    def back(self, rows, unused):
        prob = self.scores[rows, :] * self.inverse
        dscore = (prob * (self.dprobs[rows, :] - self.delta)).astype(jnp.bfloat16)
        self.acc[:HEAD, rows] += mm(self.query_t, dscore, NT)
        self.acc[HEAD:, rows] += mm(self.grad_t, prob.astype(jnp.bfloat16), NT)
        self.sums[HEAD:, :] += mm(self.kvt[:HEAD, rows], dscore)
        return unused

    def ended(self, unused):
        both = jnp.concatenate([self.out, self.sums[HEAD:, :] * HEAD ** (-0.5)], axis=0)
        self.both = both.T.astype(jnp.bfloat16)


def attend_blocks(qgs, scores, dprobs, sums, kv, kvt, acc, valid, tile):
    count = len(qgs)
    padded = kv.shape[0]
    blocks = []
    for step in range(count + 2):
        if step < count:
            blocks.append(
                Block(qgs[step], step % 3, kv, kvt, acc, scores, dprobs, sums, valid)
            )
        work = []
        if 0 <= step - 2 < count:
            work.append((blocks[step - 2].back, blocks[step - 2].ended, 0.0))
        if 0 <= step - 1 < count:
            work.append((blocks[step - 1].attend, blocks[step - 1].attended, 0.0))
        if step < count:
            work.append((blocks[step].score, blocks[step].scored, NEG))

        def body(k, carried, work=work):
            rows = pl.ds(pl.multiple_of(k * tile, tile), tile)
            return tuple(one[0](rows, held) for one, held in zip(work, carried))

        found = lax.fori_loop(
            0,
            padded // tile,
            body,
            tuple(jnp.full((8, block_rows(qgs)), one[2], jnp.float32) for one in work),
        )
        for one, held in zip(work, found):
            one[1](held)
    return [block.both for block in blocks]


def block_rows(qgs):
    return qgs[0].shape[0]


def first_kernel(
    counts_ref, index_ref, kv_ref, qg_ref, *refs, valid, tile
):
    pair = qg_ref.shape[0]
    outs, (kv, kvt, acc, wide, scores, dprobs, sums) = refs[:-7], refs[-7:]

    @pl.when(pl.program_id(0) == 0)
    def _():
        pack_tokens(counts_ref, index_ref, kv_ref, wide, kv, kvt, valid, tile)
        acc[...] = jnp.zeros(acc.shape, jnp.float32)

    found = attend_blocks(
        [qg_ref[k] for k in range(pair)], scores, dprobs, sums, kv, kvt, acc, valid, tile
    )
    for k in range(pair):
        outs[0][k] = found[k]
        outs[1 + k][...] = found[k]


def later_kernel(counts_ref, index_ref, kv, kvt, acc_ref, qg_ref, *refs, valid, tile):
    *outs, out_ref, acc, wide, scores, dprobs, sums = refs

    @pl.when(pl.program_id(0) == 0)
    def _():
        acc[...] = acc_ref[...]

    pair = qg_ref.shape[0]
    found = attend_blocks(
        [qg_ref[k] for k in range(pair)], scores, dprobs, sums, kv, kvt, acc, valid, tile
    )
    for k in range(pair):
        outs[0][k] = found[k]
        outs[1 + k][...] = found[k]

    @pl.when(pl.program_id(0) == pl.num_programs(0) - 1)
    def _():
        unpack_tokens(counts_ref, index_ref, acc, wide, out_ref, tile)


def attention_first(counts, index, kv, qg, valid, block, tile=1280):
    sources, slot, width = kv.shape
    blocks = qg.shape[0]
    padded = -(-valid // 128) * 128
    room = padded + slot + 16
    shapes = [
        jax.ShapeDtypeStruct((padded, width), jnp.bfloat16),
        jax.ShapeDtypeStruct((width, padded), jnp.bfloat16),
        jax.ShapeDtypeStruct((width, padded), jnp.float32),
    ]
    out_shape = jax.ShapeDtypeStruct((blocks, block, width), jnp.bfloat16)
    pair = blocks
    out_spec = pl.BlockSpec((pair, block, width), lambda i, c, at: (i, 0, 0))
    alone = [jax.ShapeDtypeStruct((block, width), jnp.bfloat16)] * blocks
    return pl.pallas_call(
        functools.partial(first_kernel, valid=valid, tile=tile),
        grid_spec=pltpu.PrefetchScalarGridSpec(
            num_scalar_prefetch=2,
            grid=(blocks // pair,),
            in_specs=[
                held_whole(),
                pl.BlockSpec((pair, block, width), lambda i, c, at: (i, 0, 0)),
            ],
            out_specs=[out_spec] + [whole(s.shape) for s in alone] + [held_whole() for s in shapes],
            scratch_shapes=[
                pltpu.VMEM((room, width), jnp.float32),
                pltpu.VMEM((3, padded, block), jnp.float32),
                pltpu.VMEM((3, padded, block), jnp.float32),
                pltpu.VMEM((3, width, block), jnp.float32),
            ],
        ),
        out_shape=[out_shape] + alone + shapes,
        cost_estimate=attention_cost(blocks * block, padded),
        name="attention_first",
    )(counts, index, in_vmem(kv), qg)


def attention_later(counts, index, packed, kv_shape, qg, valid, at, block, tile=1280):
    blocks, _, width = qg.shape
    padded, pair = packed[0].shape[0], blocks
    out_shape = [
        jax.ShapeDtypeStruct((blocks, block, width), jnp.bfloat16),
        *[jax.ShapeDtypeStruct((block, width), jnp.bfloat16)] * blocks,
        jax.ShapeDtypeStruct(kv_shape, jnp.bfloat16),
    ]
    return pl.pallas_call(
        functools.partial(later_kernel, valid=valid, tile=tile),
        grid_spec=pltpu.PrefetchScalarGridSpec(
            num_scalar_prefetch=2,
            grid=(blocks // pair,),
            in_specs=[held_whole() for part in packed]
            + [pl.BlockSpec((pair, block, width), lambda i, c, b: (i, at, 0))],
            out_specs=[
                pl.BlockSpec((pair, block, width), lambda i, c, b: (i, 0, 0)),
                *[whole((block, width))] * blocks,
                whole(kv_shape),
            ],
            scratch_shapes=[
                pltpu.VMEM(packed[2].shape, jnp.float32),
                pltpu.VMEM((padded + kv_shape[1] + 16, width), jnp.float32),
                pltpu.VMEM((3, padded, block), jnp.float32),
                pltpu.VMEM((3, padded, block), jnp.float32),
                pltpu.VMEM((3, width, block), jnp.float32),
            ],
        ),
        out_shape=out_shape,
        cost_estimate=attention_cost(blocks * block, padded),
        name="attention_later",
    )(counts, index, *packed, qg)


def attention_cost(rows, padded):
    return pl.CostEstimate(
        flops=24 * rows * padded * 256,
        transcendentals=rows * padded,
        bytes_accessed=8 * padded * 2 * HEAD,
    )


def side_by_side(part, heads, first):
    lanes = slice(0, HEAD) if first else slice(HEAD, 2 * HEAD)
    return jnp.concatenate([part[h][:, lanes] for h in range(heads)], axis=1)


def token_grad_kernel(dkv_ref, key_w_ref, value_w_ref, out_ref, acc, *, heads):
    step = pl.program_id(0)

    @pl.when(step == 0)
    def _():
        acc[...] = jnp.zeros(acc.shape, jnp.float32)

    part = [dkv_ref[h, step] for h in range(heads)]
    keys = side_by_side(part, heads, True)
    values = side_by_side(part, heads, False)
    acc[...] += mm(keys, key_w_ref[...], NT) + mm(values, value_w_ref[...], NT)

    @pl.when(step == pl.num_programs(0) - 1)
    def _():
        out_ref[...] = acc[...].astype(jnp.bfloat16)


def token_grad(dkv, weight):
    heads, groups, rows, pair = dkv.shape
    width = weight.shape[0]
    cols = heads * HEAD
    return pl.pallas_call(
        functools.partial(token_grad_kernel, heads=heads),
        grid=(groups,),
        in_specs=[
            held_whole(),
            pl.BlockSpec((width, cols), lambda n: (0, n)),
            pl.BlockSpec((width, cols), lambda n: (0, n + groups)),
        ],
        out_specs=whole((rows, width)),
        out_shape=jax.ShapeDtypeStruct((rows, width), jnp.bfloat16),
        scratch_shapes=[pltpu.VMEM((rows, width), jnp.float32)],
        name="token_grad",
    )(in_vmem(dkv), weight, weight)


def latent_grad_kernel(index_ref, *refs, heads, groups, by_slot):
    parts, w_ref = refs[:heads if by_slot else groups], refs[heads if by_slot else groups]
    out_ref, grad_ref = refs[-2:]
    cols = heads * HEAD
    total = None
    for k in range(groups):
        if by_slot:
            part = [chosen([ref[k] for ref in parts], h, index_ref[1]) for h in range(heads)]
        else:
            part = [parts[k][h ^ index_ref[1]] for h in range(heads)]
        at = pl.multiple_of((index_ref[0] ^ k) * cols, cols)
        out_ref[:, pl.ds(at, cols)] = side_by_side(part, heads, True)
        term = mm(side_by_side(part, heads, False), w_ref[:, pl.ds(at, cols)], NT)
        total = term if total is None else total + term
    grad_ref[...] = total.astype(jnp.bfloat16)


def chosen(part, h, flip):
    low = jnp.where(flip % 2 == 1, part[h ^ 1], part[h])
    high = jnp.where(flip % 2 == 1, part[h ^ 3], part[h ^ 2])
    return jnp.where(flip // 2 == 1, high, low)


def latent_grad(index, parts, weight, chunk, chunks, earlier, by_slot):
    groups, heads = 4, 4
    rows = parts[0].shape[-2]
    width = weight.shape[0]
    shape = jax.ShapeDtypeStruct((rows * chunks, width), jnp.bfloat16)
    out_spec = pl.BlockSpec((rows, width), lambda i, at: (chunk, 0))
    return pl.pallas_call(
        functools.partial(
            latent_grad_kernel, heads=heads, groups=groups, by_slot=by_slot
        ),
        grid_spec=pltpu.PrefetchScalarGridSpec(
            num_scalar_prefetch=1,
            grid=(1,),
            in_specs=[held_whole()] * (len(parts) + 1)
            + [pl.BlockSpec(memory_space=pl.ANY)] * len(earlier),
            out_specs=[out_spec, out_spec],
        ),
        out_shape=[shape, shape],
        input_output_aliases={2 + len(parts) + k: k for k in range(len(earlier))},
        name="latent_grad",
    )(index, *[in_vmem(part) for part in parts], weight, *earlier)


def weight_grad_kernel(*refs, slots):
    out_ref, one_ref, two_ref = refs[-1], refs[slots], refs[slots + 1]
    rows = two_ref.shape[1]
    total = None
    for k in range(slots):
        low = one_ref[k].astype(jnp.float32).T[HEAD:, :].astype(jnp.bfloat16)
        term = mm(low, refs[k][:rows, :])
        total = term if total is None else total + term
        low = two_ref[k].astype(jnp.float32).T[HEAD:, :].astype(jnp.bfloat16)
        total = total + mm(low, refs[k][rows:, :])
    out_ref[...] = total.astype(jnp.bfloat16)


def weight_grad(latents, one, two):
    return pl.pallas_call(
        functools.partial(weight_grad_kernel, slots=len(latents)),
        out_shape=jax.ShapeDtypeStruct((HEAD, latents[0].shape[1]), jnp.bfloat16),
        name="weight_grad",
    )(*latents, one, two)


def turn_kernel(index_ref, *refs):
    out_ref, scratch = refs[-2:]
    for k, ref in enumerate(refs[:-2]):
        at = pl.multiple_of((index_ref[1] ^ k) * HEAD, HEAD)
        scratch[pl.ds(at, HEAD), :] = ref[...].astype(jnp.float32)
    out_ref[...] = scratch[...].T.astype(jnp.bfloat16)


def turn(index, parts):
    width = parts[0].shape[1]
    cols = HEAD * len(parts)
    return pl.pallas_call(
        turn_kernel,
        grid_spec=pltpu.PrefetchScalarGridSpec(
            num_scalar_prefetch=1,
            grid=(1,),
            in_specs=[held_whole()] * len(parts),
            out_specs=pl.BlockSpec((width, cols), lambda i, at: (0, 0)),
            scratch_shapes=[pltpu.VMEM((cols, width), jnp.float32)],
        ),
        out_shape=jax.ShapeDtypeStruct((width, cols), jnp.bfloat16),
        name="turn",
    )(index, *[in_vmem(part) for part in parts])


def swapped(shard, axis, bit):
    return lax.ppermute(shard, axis, [(i, i ^ bit) for i in range(lax.axis_size(axis))])


def exchanged(slots, axis):
    return [slots[0]] + [
        swapped(slots[k], axis, k) for k in range(1, lax.axis_size(axis))
    ]


def gathered(shard, axis):
    near = swapped(shard, axis, 1)
    far = swapped(shard, axis, 2)
    return [shard, near, far, swapped(far, axis, 1)]


def by_head(tokens, latents, cotangent, query_weight, keyvalue_weight, counts):
    blocks = lax.axis_size("blk")
    groups = lax.axis_size("narrow")
    everyone = ("blk", "narrow")
    tok_rows, width = tokens.shape
    latent_rows = latents.shape[0]
    chunks = 2
    valid = tok_rows * groups * 614 // 1024 * blocks
    index = jnp.stack([lax.axis_index("narrow"), lax.axis_index("blk")]).astype(jnp.int32)
    pairs = project_pairs(tokens, keyvalue_weight, groups)
    pairs = pairs.reshape(blocks * groups, tok_rows, 2 * HEAD)
    held, pairs = lax.optimization_barrier((latents, pairs))
    pairs = lax.all_to_all(pairs, everyone, 0, 0, tiled=True)
    qg = project_queries(held, query_weight, cotangent, index, counts.reshape(groups), groups)
    qg = jnp.stack(exchanged(qg, "blk"))
    all_counts = qg[:, latent_rows, :groups].astype(jnp.int32)
    half = latent_rows // chunks
    held, qg = lax.optimization_barrier((latents, qg))
    far = swapped(held, "blk", 2)
    found = attention_first(all_counts, index, pairs, qg, valid, half)
    one, ones, packed = found[0], found[1:1 + blocks], found[1 + blocks:]
    near_one, far_one = swapped(one, "narrow", 1), swapped(one, "narrow", 2)
    two, *twos, dkv = attention_later(
        all_counts, index, packed, pairs.shape, qg, valid, 1, half
    )
    dkv, ones, twos, near_one, far_one, far = lax.optimization_barrier(
        (dkv, ones, twos, near_one, far_one, far)
    )
    every = [latents, swapped(latents, "blk", 1), far, swapped(far, "blk", 1)]
    last_one = swapped(far_one, "narrow", 1)
    dkv = lax.all_to_all(dkv, everyone, 0, 0, tiled=True)
    own_two = jnp.stack(exchanged(twos, "blk"))
    own_two, every, two = lax.optimization_barrier((own_two, every, two))
    part_two = gathered(own_two, "narrow")
    by_slot = [
        jnp.stack([ones[k], near_one[k], far_one[k], last_one[k]]) for k in range(blocks)
    ]
    part_one = exchanged(by_slot, "blk")
    grad_query_weight = turn(index, gathered(weight_grad(every, one, two), "blk"))
    done = latent_grad(index, part_one, query_weight, 0, chunks, (), True)
    done, dkv = lax.optimization_barrier((done, dkv))
    grad_tokens = token_grad(
        dkv.reshape(blocks, groups, tok_rows, 2 * HEAD), keyvalue_weight
    )
    done, part_two, grad_tokens = lax.optimization_barrier((done, part_two, grad_tokens))
    latent_out, grad_latents = latent_grad(
        index, part_two, query_weight, 1, chunks, done, False
    )
    return (latent_out, grad_latents, grad_query_weight, grad_tokens)


def on_device(tokens, latents, cotangent, query_weight, keyvalue_weight, counts):
    narrow_size = lax.axis_size("narrow")
    narrow_index = lax.axis_index("narrow")
    tok_rows = tokens.shape[0]
    model_width = tokens.shape[1]
    share = model_width // narrow_size
    queries = jnp.dot(latents, query_weight, preferred_element_type=jnp.float32).astype(
        jnp.bfloat16
    )
    pairs = jnp.dot(tokens, keyvalue_weight, preferred_element_type=jnp.float32).astype(
        jnp.bfloat16
    )
    key_heads = pairs[:, :model_width].reshape(tok_rows, HEADS, HEAD)
    value_heads = pairs[:, model_width:].reshape(tok_rows, HEADS, HEAD)
    valid_mask = jnp.arange(tok_rows) < counts[0, narrow_index]
    row_max, row_sum, weighted, visited = forward_cycle(queries, key_heads, value_heads, valid_mask)
    row_max, row_sum, weighted = merged_2((row_max, row_sum, weighted), "narrow", join_partials)
    heads_here = row_max.shape[0]
    latent_rows = weighted.shape[0]
    attended = weighted.reshape(latent_rows, heads_here, HEAD) / row_sum.T[:, :, None]
    attended_low = attended.reshape(latent_rows, -1).astype(jnp.bfloat16)
    delta = jnp.sum(
        cotangent.astype(jnp.float32).reshape(latent_rows, heads_here, HEAD) * attended, axis=2
    ).T
    log_total = row_max + jnp.log(row_sum)
    query_grad, key_grad, value_grad = backward_cycle(
        visited, cotangent, log_total, delta, key_heads, value_heads, valid_mask
    )
    pair_grad = jnp.concatenate([key_grad, value_grad], axis=1).astype(jnp.bfloat16)
    query_part = lax.psum_scatter(query_grad, "narrow", scatter_dimension=1, tiled=True)
    query_low = query_part.astype(jnp.bfloat16)
    weight_cols = lax.dynamic_slice_in_dim(query_weight, narrow_index * share, share, 1)
    weight_term = lax.dot_general(
        latents, query_low, (((0,), (0,)), ((), ())), preferred_element_type=jnp.float32
    )
    grad_query_weight = lax.psum(weight_term, "blk").astype(jnp.bfloat16)
    latent_term = lax.dot_general(
        query_low, weight_cols, (((1,), (1,)), ((), ())), preferred_element_type=jnp.float32
    )
    grad_latents = lax.psum(latent_term, "narrow").astype(jnp.bfloat16)
    grad_tokens = lax.dot_general(
        pair_grad, keyvalue_weight, (((1,), (1,)), ((), ())), preferred_element_type=jnp.float32
    ).astype(jnp.bfloat16)
    return (attended_low, grad_latents, grad_query_weight, grad_tokens)


def solution(mesh):
    placed = (
        P(("groups", "blk", "narrow"), None),
        P("blk", None),
        P(("groups", "blk"), None),
        P(),
        P(),
        P(("groups", "blk"), None),
    )
    one_head_each = mesh.shape["blk"] == 4 and mesh.shape["narrow"] == 4
    return jax.shard_map(
        by_head if one_head_each else on_device,
        mesh=mesh,
        in_specs=placed,
        out_specs=(
            P(("groups", "blk"), None),
            P(("groups", "blk"), None),
            P("groups", "narrow"),
            P(("groups", "blk", "narrow"), None),
        ),
        check_vma=False,
    )
```
